32 devices in a mesh: groups: 2 (over x), rows: 16 (over z, y, core).
Axes of the slice: x: 2, y: 2, z: 4, core: 2. Of those that a mesh axis runs over, the one named last changes fastest.
Arguments:
- block_input: bfloat16 [512, 352, 512], P(('groups', 'rows')), parts along dimension 0, may hold values from -6 to 6
- first_pre: bfloat16 [512, 352, 128], P(('groups', 'rows')), parts along dimension 0, may hold values from -6 to 6
- second_pre: bfloat16 [512, 352, 128], P(('groups', 'rows')), parts along dimension 0, may hold values from -6 to 6
- output_pre: bfloat16 [512, 352, 512], P(('groups', 'rows')), parts along dimension 0, may hold values from -6 to 6
- output_grad: bfloat16 [512, 352, 512], P('groups', None, 'rows'), parts along dimension 0, may hold values from -6 to 6
- first_weight: bfloat16 [512, 128], replicated, may hold values from -0.25 to 0.25
- middle_weight: bfloat16 [3, 3, 128, 128], replicated, may hold values from -0.1875 to 0.1875
- last_weight: bfloat16 [128, 512], replicated, may hold values from -0.5 to 0.5
Outputs:
- input_grad: bfloat16 [512, 352, 512], P(('groups', 'rows')), parts along dimension 0
- first_weight_grad: float32 [1024, 128], P(('groups', 'rows')), parts along dimension 0
- middle_weight_grad: float32 [6, 3, 128, 128], P('groups'), parts along dimension 0
- last_weight_grad: float32 [256, 512], P('groups'), parts along dimension 0
The draws below stay inside these ranges and needn't reach their ends.
There are 2 independent parts, one for each index of `groups`. The reference program is written for one: setup_inputs(seed, part) draws one part's arguments, and reference() takes and returns one part's arrays. A program takes and returns all parts, laid end to end along the dimension named above; an argument that names none is the same for every part. Nothing has to cross between parts.
All inputs are finite; a program needn't handle non-finite values.
Results may differ from the reference program's by a relative error of at most 0.0049.
Values may be sent and summed in bfloat16 or wider, within the bound.
No kernel may reach another device: no remote copies, remote signals or barrier semaphores. Data moves between devices by JAX's collectives and lax.ppermute only.
A program may use at most 128 MiB of HBM per device.

```python
import math
import jax
import jax.numpy as jnp
from jax import lax

C = 512
CM = 128
COLS = 352
HEIGHT = 256


def shard_levels(rng, extent, pieces, low, top_value):
    def one(dim, blocks):
        draws = jax.random.uniform(jax.random.fold_in(jax.random.fold_in(rng, 6), dim), (blocks,), jnp.float32, low / len(pieces), top_value / len(pieces))
        return jnp.repeat(jnp.exp(draws), extent[dim] // blocks).reshape((-1,) + (1,) * (len(extent) - dim - 1))

    factor_of = one(*pieces[0])
    for cut in pieces[1:]:
        factor_of = factor_of * one(*cut)
    return factor_of


def gaussian(stream_key, shape, scale, most, shards=(), dtype=jnp.bfloat16):
    gain = shard_levels(stream_key, shape, shards, -0.22, 0.18) if shards else 1.0
    entries = jax.random.normal(stream_key, shape, jnp.float32) * scale * gain
    return jnp.minimum(jnp.maximum(entries, -most), most).astype(dtype)


def setup_inputs(seed: int = 0, part: int = 0) -> dict:
    seeds = jax.random.split(jax.random.key(seed), 9)
    part_splits = jax.random.split(jax.random.fold_in(seeds[8], part), 9)
    return {
        "block_input": gaussian(part_splits[0], (HEIGHT, COLS, C), 1.0, 6.0, ((0, 16),)),
        "first_pre": gaussian(part_splits[1], (HEIGHT, COLS, CM), 1.0, 6.0, ((0, 16),)),
        "second_pre": gaussian(part_splits[2], (HEIGHT, COLS, CM), 1.0, 6.0, ((0, 16),)),
        "output_pre": gaussian(part_splits[3], (HEIGHT, COLS, C), 1.0, 6.0, ((0, 16),)),
        "output_grad": gaussian(part_splits[4], (HEIGHT, COLS, C), 1.0, 6.0, ((2, 16),)),
        "first_weight": gaussian(seeds[5], (C, CM), C ** -0.5, 0.25),
        "middle_weight": gaussian(seeds[6], (3, 3, CM, CM), (9 * CM) ** -0.5, 0.1875),
        "last_weight": gaussian(seeds[7], (CM, C), CM ** -0.5, 0.5),
    }


def contract_rows(left, right):
    return lax.dot_general(left, right, (((0,), (0,)), ((), ())), preferred_element_type=jnp.float32)

def reference(block_input, first_pre, second_pre, output_pre, output_grad, first_weight, middle_weight, last_weight):
    map_rows, map_cols, channels = block_input.shape
    inner_width = first_pre.shape[2]
    pixels = map_rows * map_cols
    factor = 1.0 / math.sqrt(pixels)
    masked_out = jnp.where(output_pre > 0, output_grad, jnp.zeros_like(output_grad))
    second_act = jnp.maximum(second_pre, jnp.zeros_like(second_pre))
    first_act = jnp.maximum(first_pre, jnp.zeros_like(first_pre))
    out_flat = masked_out.reshape(pixels, channels)
    last_grad = contract_rows(second_act.reshape(pixels, inner_width), out_flat) * factor
    inner = lax.dot_general(out_flat, last_weight, (((1,), (1,)), ((), ())), preferred_element_type=jnp.float32)
    second_grad = jnp.where(second_pre.reshape(pixels, inner_width) > 0, inner, 0.0).astype(jnp.bfloat16)
    second_grad = second_grad.reshape(map_rows, map_cols, inner_width)
    act_padded = jnp.pad(first_act, ((1, 1), (1, 1), (0, 0)))
    grad_padded = jnp.pad(second_grad, ((1, 1), (1, 1), (0, 0)))
    second_flat = second_grad.reshape(pixels, inner_width)
    taps = []
    total = jnp.zeros((pixels, inner_width), jnp.float32)
    for row_tap in range(3):
        line = []
        for col_tap in range(3):
            window = act_padded[row_tap:row_tap + map_rows, col_tap:col_tap + map_cols].reshape(pixels, inner_width)
            line.append(contract_rows(window, second_flat))
            moved = grad_padded[2 - row_tap:2 - row_tap + map_rows, 2 - col_tap:2 - col_tap + map_cols].reshape(pixels, inner_width)
            total = total + lax.dot_general(moved, middle_weight[row_tap, col_tap], (((1,), (1,)), ((), ())), preferred_element_type=jnp.float32)
        taps.append(jnp.stack(line))
    middle_grad = jnp.stack(taps) * factor
    first_grad = jnp.where(first_pre.reshape(pixels, inner_width) > 0, total, 0.0).astype(jnp.bfloat16)
    first_wgrad = contract_rows(block_input.reshape(pixels, channels), first_grad) * factor
    back = lax.dot_general(first_grad, first_weight, (((1,), (1,)), ((), ())), preferred_element_type=jnp.float32)
    input_grad = (back + out_flat.astype(jnp.float32)).astype(jnp.bfloat16).reshape(map_rows, map_cols, channels)
    return (input_grad, first_wgrad, middle_grad, last_grad)
```

```python
import functools
import math

import jax
import jax.numpy as jnp
from jax import lax
from jax.experimental import pallas as pl
from jax.experimental.pallas import tpu as pltpu
from jax.sharding import PartitionSpec as P

BF = jnp.bfloat16
F32 = jnp.float32
AXIS = "rows"
BLK = 16
LANES = 128


def dims(lhs, rhs):
    return (((lhs,), (rhs,)), ((), ()))


def mm(a, b):
    return lax.dot_general(a, b, dims(1, 0), preferred_element_type=F32)


def mm_nt(a, b):
    return lax.dot_general(a, b, dims(1, 1), preferred_element_type=F32)


def unit(count, offset, cap):
    return max(u for u in range(1, cap + 1) if count % u == 0 and offset % u == 0)


def params():
    return pltpu.CompilerParams(
        dimension_semantics=("arbitrary",), vmem_limit_bytes=48 * 2**20
    )


def cost(flops, nbytes):
    return pl.CostEstimate(flops=int(flops), transcendentals=0, bytes_accessed=int(nbytes))


def whole(shape):
    zeros = (0,) * len(shape)
    return pl.BlockSpec(shape, lambda i: zeros)


def eye(size):
    a = lax.broadcasted_iota(jnp.int32, (size, size), 0)
    b = lax.broadcasted_iota(jnp.int32, (size, size), 1)
    return (a == b).astype(BF)


def pack_kernel(tile_rows, units, groups, x_ref, eye_ref, out_ref):
    side = eye_ref.shape[0]
    per = side // tile_rows
    depth = groups * LANES
    for u in range(units):
        for h in range(x_ref.shape[1] // side):
            part = x_ref[u * depth : (u + 1) * depth, h * side : (h + 1) * side]
            turned = mm_nt(eye_ref[...], part).astype(BF)
            for g in range(groups):
                piece = turned[:, g * LANES : (g + 1) * LANES]
                out_ref[
                    h * per : (h + 1) * per, u, g * tile_rows : (g + 1) * tile_rows, :
                ] = piece.reshape(per, tile_rows, LANES)


def pack(x, count, tile_rows, groups, start, blocks):
    depth = groups * LANES
    height = x.shape[1]
    side = 256 if height % 256 == 0 else LANES
    u = unit(blocks, start, 4)
    first = start // u
    return pl.pallas_call(
        functools.partial(pack_kernel, tile_rows, u, groups),
        grid=(blocks // u,),
        in_specs=[
            pl.BlockSpec((u * depth, height), lambda i: (first + i, 0)),
            whole((side, side)),
        ],
        out_specs=pl.BlockSpec(
            (count, u, groups * tile_rows, LANES), lambda i: (0, i, 0, 0)
        ),
        out_shape=jax.ShapeDtypeStruct((count, blocks, groups * tile_rows, LANES), BF),
        compiler_params=params(),
        cost_estimate=cost(
            2 * height * side * blocks * depth, 4 * blocks * depth * height
        ),
        name="pack",
    )(x, eye(side))


def open_kernel(units, join, alias, *refs):
    if alias:
        refs = refs[1:]
    (recv, opre, spre, lanes_ref, pixels_ref, weight, lw_in, buf, sg, lw) = refs
    rows = opre.shape[0]
    tiles = recv.shape[0] // join
    height = recv.shape[2]
    pixels = rows * BLK

    @pl.when(pl.program_id(0) == 0)
    def _():
        lw[...] = lw_in[...]

    for u in range(units):
        stack = jnp.concatenate(
            [
                jnp.concatenate([recv[t * join + s, u] for s in range(join)], axis=1)
                for t in range(tiles)
            ],
            axis=0,
        )
        sorted_lanes = mm(stack, lanes_ref[...]).astype(BF)
        by_pixel = jnp.concatenate(
            [
                jnp.concatenate(
                    [
                        sorted_lanes[
                            t * height : (t + 1) * height, j * LANES : (j + 1) * LANES
                        ]
                        for t in range(tiles)
                    ],
                    axis=1,
                )
                for j in range(join)
            ],
            axis=0,
        )
        spatial = mm(pixels_ref[...], by_pixel)
        cols = slice(u * BLK, (u + 1) * BLK)
        gate = opre[:, cols, :].reshape(pixels, tiles * LANES).astype(F32) > 0
        masked = jnp.where(gate, spatial, 0.0).astype(BF)
        buf[:, cols, :] = masked.reshape(rows, BLK, tiles * LANES)
        pre = spre[:, cols, :].reshape(pixels, LANES).astype(F32)
        inner = mm_nt(masked, weight[...])
        sg[:, cols, :] = (
            jnp.where(pre > 0, inner, 0.0).astype(BF).reshape(rows, BLK, LANES)
        )
        act = jnp.maximum(pre, 0.0).astype(BF)
        part = mm(jnp.transpose(act), masked)
        for t in range(tiles):
            lw[t] += part[:, t * LANES : (t + 1) * LANES]


def open_block(buf, recv, opre, spre, lane_sort, pixel_sort, weight, lw_in, join, start):
    rows, _, channels = opre.shape
    count, blocks, height, _ = recv.shape
    tiles = channels // LANES
    u = unit(blocks, start, 2)
    first = start // u
    alias = buf is not None
    wide = lambda c: pl.BlockSpec((rows, u * BLK, c), lambda i: (0, first + i, 0))
    pixels = rows * BLK * blocks
    call = pl.pallas_call(
        functools.partial(open_kernel, u, join, alias),
        grid=(blocks // u,),
        in_specs=([pl.BlockSpec(memory_space=pl.ANY)] if alias else [])
        + [
            pl.BlockSpec((count, u, height, LANES), lambda i: (0, i, 0, 0)),
            wide(channels),
            wide(LANES),
            whole(lane_sort.shape),
            whole(pixel_sort.shape),
            whole(weight.shape),
            whole(lw_in.shape),
        ],
        out_specs=[
            wide(channels),
            pl.BlockSpec((rows, u * BLK, LANES), lambda i: (0, i, 0)),
            whole(lw_in.shape),
        ],
        out_shape=[
            jax.ShapeDtypeStruct(opre.shape, BF),
            jax.ShapeDtypeStruct((rows, blocks * BLK, LANES), BF),
            jax.ShapeDtypeStruct(lw_in.shape, F32),
        ],
        input_output_aliases={0: 0} if alias else {},
        compiler_params=params(),
        cost_estimate=cost(
            2 * pixels * channels * (512 + 256 + 256), 2 * pixels * (3 * channels + 256)
        ),
        name="open_block",
    )
    args = (recv, opre, spre, lane_sort, pixel_sort, weight, lw_in)
    return call(*(((buf,) + args) if alias else args))


def middle_kernel(units, last, sg, act, start_ref, out, total):
    step = pl.program_id(0)
    rows = sg.shape[0]
    pixels = rows * BLK

    @pl.when(step == 0)
    def _():
        total[...] = start_ref[...]

    for u in range(units):
        cols = slice(u * BLK, (u + 1) * BLK)
        turned = jnp.transpose(sg[:, cols, :].reshape(pixels, LANES))
        for a in range(3):
            window = act[a : a + rows, cols, :].reshape(pixels, 3 * LANES)
            total[a] += mm(turned, window)

    @pl.when(step == pl.num_programs(0) - 1)
    def _():
        if last:
            for a in range(3):
                for b in range(3):
                    out[a, b] = jnp.transpose(total[a, :, b * LANES : (b + 1) * LANES])
        else:
            out[...] = total[...]


def middle(sg, act, start, last):
    rows, width, _ = sg.shape
    blocks = width // BLK
    u = unit(blocks, 0, 4)
    shape = (3, 3, LANES, LANES) if last else (3, LANES, 3 * LANES)
    return pl.pallas_call(
        functools.partial(middle_kernel, u, last),
        grid=(blocks // u,),
        in_specs=[
            pl.BlockSpec((rows, u * BLK, LANES), lambda i: (0, i, 0)),
            pl.BlockSpec((rows + 2, u * BLK, 3 * LANES), lambda i: (0, i, 0)),
            whole(start.shape),
        ],
        out_specs=whole(shape),
        out_shape=jax.ShapeDtypeStruct(shape, F32),
        scratch_shapes=[pltpu.VMEM((3, LANES, 3 * LANES), F32)],
        compiler_params=params(),
        cost_estimate=cost(
            2 * rows * width * 9 * LANES * LANES, rows * width * 2 * 4 * LANES
        ),
        name="middle",
    )(sg, act, start)


def close_kernel(units, last, buf_in, sg, taps, fpre, binput, weight, fw_in, buf, fw, total):
    step = pl.program_id(0)
    rows = fpre.shape[0]
    pixels = rows * BLK
    channels = binput.shape[2]

    @pl.when(step == 0)
    def _():
        total[...] = fw_in[...]

    for u in range(units):
        cols = slice(u * BLK, (u + 1) * BLK)
        acc = None
        for a in range(3):
            moved = sg[2 - a : 2 - a + rows, cols, :].reshape(pixels, 3 * LANES)
            part = mm(moved, taps[a])
            acc = part if acc is None else acc + part
        gate = fpre[:, cols, :].reshape(pixels, LANES).astype(F32) > 0
        grad = jnp.where(gate, acc, 0.0).astype(BF)
        total[...] += mm(
            jnp.transpose(grad), binput[:, cols, :].reshape(pixels, channels)
        )
        back = mm_nt(grad, weight[...])
        direct = buf_in[:, cols, :].reshape(pixels, channels).astype(F32)
        buf[:, cols, :] = (back + direct).astype(BF).reshape(rows, BLK, channels)

    @pl.when(step == pl.num_programs(0) - 1)
    def _():
        if last:
            for t in range(channels // LANES):
                fw[t * LANES : (t + 1) * LANES, :] = jnp.transpose(
                    total[:, t * LANES : (t + 1) * LANES]
                )
        else:
            fw[...] = total[...]


def close_block(buf, sg, taps, fpre, binput, weight, fw_in, start, last):
    rows, _, channels = binput.shape
    width = sg.shape[1]
    blocks = width // BLK
    u = unit(blocks, start, 3)
    first = start // u
    wide = lambda c: pl.BlockSpec((rows, u * BLK, c), lambda i: (0, first + i, 0))
    shape = (channels, LANES) if last else (LANES, channels)
    pixels = rows * width
    return pl.pallas_call(
        functools.partial(close_kernel, u, last),
        grid=(blocks // u,),
        in_specs=[
            wide(channels),
            pl.BlockSpec((rows + 2, u * BLK, 3 * LANES), lambda i: (0, i, 0)),
            whole(taps.shape),
            wide(LANES),
            wide(channels),
            whole(weight.shape),
            whole(fw_in.shape),
        ],
        out_specs=[wide(channels), whole(shape)],
        out_shape=[
            jax.ShapeDtypeStruct(buf.shape, BF),
            jax.ShapeDtypeStruct(shape, F32),
        ],
        scratch_shapes=[pltpu.VMEM((LANES, channels), F32)],
        input_output_aliases={0: 0},
        compiler_params=params(),
        cost_estimate=cost(
            2 * pixels * LANES * (9 * LANES + 2 * channels),
            2 * pixels * (3 * channels + 4 * LANES),
        ),
        name="close_block",
    )(buf, sg, taps, fpre, binput, weight, fw_in)


def swap_pairs(value, count):
    return lax.ppermute(value, AXIS, [(i, i ^ 1) for i in range(count)])


def same_core(count):
    return [list(range(c, count, 2)) for c in range(2)]


def scatter_sum(parts, count):
    odd = lax.axis_index(AXIS) % 2 == 1
    pairs = parts.reshape((count // 2, 2) + parts.shape[1:])
    kept = jnp.where(odd, pairs[:, 1], pairs[:, 0])
    given = jnp.where(odd, pairs[:, 0], pairs[:, 1])
    both = kept + swap_pairs(given, count)
    got = lax.all_to_all(
        both, AXIS, 0, 0, tiled=True, axis_index_groups=same_core(count)
    )
    return jnp.sum(got, axis=0)


def gather(share, count):
    odd = lax.axis_index(AXIS) % 2 == 1
    copies = jnp.broadcast_to(share[None], (count // 2,) + share.shape)
    own = lax.all_to_all(
        copies, AXIS, 0, 0, tiled=True, axis_index_groups=same_core(count)
    )
    other = swap_pairs(own, count)
    pairs = jnp.stack([jnp.where(odd, other, own), jnp.where(odd, own, other)], axis=1)
    return pairs.reshape((count * share.shape[0],) + share.shape[1:])


def edges(value, count):
    up = [(i, i + 1) for i in range(count - 1)]
    down = [(i + 1, i) for i in range(count - 1)]
    return lax.ppermute(value[-1:], AXIS, up), lax.ppermute(value[:1], AXIS, down)


def beside(value):
    width = value.shape[1] - 2
    return [value[:, b : b + width] for b in range(3)]


def shards(
    block_input,
    first_pre,
    second_pre,
    output_pre,
    output_grad,
    first_weight,
    middle_weight,
    last_weight,
):
    tile_rows, map_cols, channels = block_input.shape
    inner = first_pre.shape[2]
    count = lax.axis_size(AXIS)
    factor = 1.0 / math.sqrt(tile_rows * map_cols * count)
    own = channels // count
    join = LANES // own
    groups = BLK // join
    blocks = map_cols // BLK
    head = 4 * (3 * blocks // 16)
    tail = blocks - head
    split = head * BLK
    seam = split - BLK

    turned = jnp.transpose(output_grad, (1, 2, 0)).reshape(map_cols * own, -1)
    send_a = pack(turned, count, tile_rows, groups, 0, head)
    recv_a = lax.all_to_all(send_a, AXIS, 0, 0, tiled=True)
    turned, _ = lax.optimization_barrier((turned, send_a))
    send_b = pack(turned, count, tile_rows, groups, head, tail)
    recv_b = lax.all_to_all(send_b, AXIS, 0, 0, tiled=True)

    size = join * LANES
    lane = jnp.arange(size)
    src, col, chan = lane // LANES, lane % LANES // own, lane % own
    lane_sort = (
        (col * LANES + src * own + chan)[:, None] == lane[None, :]
    ).astype(BF)
    pixel = jnp.arange(tile_rows * BLK)
    row, column = pixel // BLK, pixel % BLK
    place = (column % join * groups + column // join) * tile_rows + row
    pixel_sort = (place[:, None] == pixel[None, :]).astype(BF)
    taps = jnp.transpose(middle_weight, (0, 1, 3, 2)).reshape(3, 3 * inner, inner)

    before, after = edges(first_pre, count)
    act = jnp.maximum(jnp.concatenate([before, first_pre, after], axis=0), 0)
    act = jnp.concatenate(beside(jnp.pad(act, ((0, 0), (1, 1), (0, 0)))), axis=2)
    act_a, act_b = act[:, :split], act[:, split:]

    lw0 = jnp.zeros((channels // LANES, inner, LANES), F32)
    buf, sg_a, lw_a = open_block(
        None, recv_a, output_pre, second_pre, lane_sort, pixel_sort, last_weight, lw0, join, 0
    )
    before, after = edges(sg_a, count)
    mw_a = middle(sg_a, act_a, jnp.zeros((3, inner, 3 * inner), F32), False)
    ext_a = jnp.concatenate([before, sg_a, after], axis=0)
    near = jnp.pad(ext_a, ((0, 0), (1, 0), (0, 0)))[:, : seam + 2]
    near = jnp.concatenate(beside(near)[::-1], axis=2)
    buf, fw_a = close_block(
        buf,
        near,
        taps,
        first_pre,
        block_input,
        first_weight,
        jnp.zeros((inner, channels), F32),
        0,
        False,
    )

    buf, sg_b, lw = open_block(
        buf, recv_b, output_pre, second_pre, lane_sort, pixel_sort, last_weight, lw_a, join, head
    )
    before, after = edges(sg_b, count)
    mw = middle(sg_b, act_b, mw_a, True)
    both = jnp.concatenate(
        [mw.reshape(9 * inner, inner), lw.reshape(channels, LANES)], axis=0
    )
    share = scatter_sum(both.reshape(count, -1, LANES), count)
    both = gather(share * factor, count)

    ext_b = jnp.concatenate([before, sg_b, after], axis=0)
    far = jnp.concatenate([ext_a[:, seam - 1 :], ext_b], axis=1)
    far = jnp.pad(far, ((0, 0), (0, 1), (0, 0)))
    far = jnp.concatenate(beside(far)[::-1], axis=2)
    buf, fw = close_block(
        buf, far, taps, first_pre, block_input, first_weight, fw_a, head - 1, True
    )
    first_wgrad = scatter_sum(fw.reshape(count, own, LANES), count) * factor

    middle_wgrad = both[: 9 * inner].reshape(3, 3, inner, inner)
    last_wgrad = (
        both[9 * inner :].reshape(-1, inner, LANES).transpose(1, 0, 2).reshape(inner, channels)
    )
    return (buf, first_wgrad, middle_wgrad, last_wgrad)


def solution(mesh):
    placed = (
        P(("groups", "rows"), None, None),
        P(("groups", "rows"), None, None),
        P(("groups", "rows"), None, None),
        P(("groups", "rows"), None, None),
        P("groups", None, "rows"),
        P(),
        P(),
        P(),
    )
    return jax.shard_map(
        shards,
        mesh=mesh,
        in_specs=placed,
        out_specs=(
            P(("groups", "rows"), None, None),
            P(("groups", "rows"), None),
            P("groups", None, None, None),
            P("groups", None),
        ),
        check_vma=False,
    )
```

```python
import functools
import math

import jax
import jax.numpy as jnp
from jax import lax
from jax.experimental import pallas as pl
from jax.experimental.pallas import tpu as pltpu
from jax.sharding import PartitionSpec as P

BF = jnp.bfloat16
F32 = jnp.float32
AXIS = "rows"
BLK = 16
LANES = 128


def dims(lhs, rhs):
    return (((lhs,), (rhs,)), ((), ()))


def mm(a, b):
    return lax.dot_general(a, b, dims(1, 0), preferred_element_type=F32)


def mm_nt(a, b):
    return lax.dot_general(a, b, dims(1, 1), preferred_element_type=F32)


def unit(count, offset, cap):
    return max(u for u in range(1, cap + 1) if count % u == 0 and offset % u == 0)


def params():
    return pltpu.CompilerParams(
        dimension_semantics=("arbitrary",), vmem_limit_bytes=24 * 2**20
    )


def hbm(value):
    return pltpu.with_memory_space_constraint(value, pltpu.HBM)


def cost(flops, nbytes):
    return pl.CostEstimate(
        flops=int(flops) // 64, transcendentals=0, bytes_accessed=int(nbytes) // 64
    )


def whole(shape):
    zeros = (0,) * len(shape)
    return pl.BlockSpec(shape, lambda i: zeros)


def eye(size):
    a = lax.broadcasted_iota(jnp.int32, (size, size), 0)
    b = lax.broadcasted_iota(jnp.int32, (size, size), 1)
    return (a == b).astype(BF)


def pack_kernel(tile_rows, units, groups, x_ref, eye_ref, out_ref):
    side = eye_ref.shape[0]
    per = side // tile_rows
    depth = groups * LANES
    for u in range(units):
        for h in range(x_ref.shape[1] // side):
            part = x_ref[u * depth : (u + 1) * depth, h * side : (h + 1) * side]
            turned = mm_nt(eye_ref[...], part).astype(BF)
            for g in range(groups):
                piece = turned[:, g * LANES : (g + 1) * LANES]
                out_ref[
                    h * per : (h + 1) * per, u, g * tile_rows : (g + 1) * tile_rows, :
                ] = piece.reshape(per, tile_rows, LANES)


def pack(x, count, tile_rows, groups, start, blocks):
    depth = groups * LANES
    height = x.shape[1]
    side = 256 if height % 256 == 0 else LANES
    u = unit(blocks, start, 4)
    first = start // u
    return pl.pallas_call(
        functools.partial(pack_kernel, tile_rows, u, groups),
        grid=(blocks // u,),
        in_specs=[
            pl.BlockSpec((u * depth, height), lambda i: (first + i, 0)),
            whole((side, side)),
        ],
        out_specs=pl.BlockSpec(
            (count, u, groups * tile_rows, LANES), lambda i: (0, i, 0, 0)
        ),
        out_shape=pltpu.HBM((count, blocks, groups * tile_rows, LANES), BF),
        compiler_params=params(),
        cost_estimate=cost(
            2 * height * side * blocks * depth, 4 * blocks * depth * height
        ),
        name="pack",
    )(hbm(x), eye(side))


def open_kernel(units, join, alias, *refs):
    if alias:
        refs = refs[1:]
    (recv, opre, spre, lanes_ref, pixels_ref, weight, lw_in, buf, sg, lw) = refs
    rows = opre.shape[0]
    tiles = recv.shape[0] // join
    height = recv.shape[2]
    pixels = rows * units * BLK

    @pl.when(pl.program_id(0) == 0)
    def _():
        lw[...] = lw_in[...]

    stack = jnp.concatenate(
        [
            jnp.concatenate([recv[t * join + s, u] for s in range(join)], axis=1)
            for u in range(units)
            for t in range(tiles)
        ],
        axis=0,
    )
    sorted_lanes = mm(stack, lanes_ref[...]).astype(BF)
    spatial = []
    for u in range(units):
        by_pixel = jnp.concatenate(
            [
                jnp.concatenate(
                    [
                        sorted_lanes[
                            (u * tiles + t) * height : (u * tiles + t + 1) * height,
                            j * LANES : (j + 1) * LANES,
                        ]
                        for t in range(tiles)
                    ],
                    axis=1,
                )
                for j in range(join)
            ],
            axis=0,
        )
        spatial.append(
            mm(pixels_ref[...], by_pixel).reshape(rows, BLK, tiles * LANES)
        )
    spatial = jnp.concatenate(spatial, axis=1).reshape(pixels, tiles * LANES)
    gate = opre[...].reshape(pixels, tiles * LANES).astype(F32) > 0
    masked = jnp.where(gate, spatial, 0.0).astype(BF)
    buf[...] = masked.reshape(buf.shape)
    pre = spre[...].reshape(pixels, LANES).astype(F32)
    inner = mm_nt(masked, weight[...])
    sg[...] = jnp.where(pre > 0, inner, 0.0).astype(BF).reshape(sg.shape)
    act = jnp.maximum(pre, 0.0).astype(BF)
    part = mm(jnp.transpose(act), masked)
    for t in range(tiles):
        lw[t] += part[:, t * LANES : (t + 1) * LANES]


def open_block(buf, recv, opre, spre, lane_sort, pixel_sort, weight, lw_in, join, start):
    rows, _, channels = opre.shape
    count, blocks, height, _ = recv.shape
    tiles = channels // LANES
    u = unit(blocks, start, 4)
    first = start // u
    alias = buf is not None
    wide = lambda c: pl.BlockSpec((rows, u * BLK, c), lambda i: (0, first + i, 0))
    pixels = rows * BLK * blocks
    call = pl.pallas_call(
        functools.partial(open_kernel, u, join, alias),
        grid=(blocks // u,),
        in_specs=([pl.BlockSpec(memory_space=pl.ANY)] if alias else [])
        + [
            pl.BlockSpec((count, u, height, LANES), lambda i: (0, i, 0, 0)),
            wide(channels),
            wide(LANES),
            whole(lane_sort.shape),
            whole(pixel_sort.shape),
            whole(weight.shape),
            whole(lw_in.shape),
        ],
        out_specs=[
            wide(channels),
            pl.BlockSpec((rows, u * BLK, LANES), lambda i: (0, i, 0)),
            whole(lw_in.shape),
        ],
        out_shape=[
            jax.ShapeDtypeStruct(opre.shape, BF),
            jax.ShapeDtypeStruct((rows, blocks * BLK, LANES), BF),
            jax.ShapeDtypeStruct(lw_in.shape, F32),
        ],
        input_output_aliases={0: 0} if alias else {},
        compiler_params=params(),
        cost_estimate=cost(
            2 * pixels * channels * (512 + 256 + 256), 2 * pixels * (3 * channels + 256)
        ),
        name="open_block",
    )
    args = (hbm(recv), hbm(opre), hbm(spre), lane_sort, pixel_sort, weight, lw_in)
    return call(*(((buf,) + args) if alias else args))


def middle_kernel(units, sg, act, start_ref, *refs):
    lw, rim, rim_act, out, total = refs if len(refs) == 5 else (None,) * 3 + refs
    step = pl.program_id(0)
    rows = sg.shape[0]
    pixels = rows * units * BLK

    @pl.when(step == 0)
    def _():
        total[...] = start_ref[...]

    turned = jnp.transpose(sg[...].reshape(pixels, LANES))
    for a in range(3):
        window = act[a : a + rows].reshape(pixels, 3 * LANES)
        total[a] += mm(turned, window)

    @pl.when(step == pl.num_programs(0) - 1)
    def _():
        if lw is None:
            out[...] = total[...]
        else:
            for e in range(2):
                total[2 - 2 * e] += mm(jnp.transpose(rim[e]), rim_act[e])
            for a in range(3):
                for b in range(3):
                    top = (3 * a + b) * LANES
                    out[top : top + LANES, :] = jnp.transpose(
                        total[a, :, b * LANES : (b + 1) * LANES]
                    )
            for t in range(lw.shape[0]):
                top = (9 + t) * LANES
                out[top : top + LANES, :] = lw[t]


def middle(sg, act, start, lw=None, rim=None, rim_act=None):
    rows, width, _ = sg.shape
    blocks = width // BLK
    u = unit(blocks, 0, 4)
    extra = () if lw is None else (lw, rim, rim_act)
    shape = start.shape if lw is None else ((9 + lw.shape[0]) * LANES, LANES)
    return pl.pallas_call(
        functools.partial(middle_kernel, u),
        grid=(blocks // u,),
        in_specs=[
            pl.BlockSpec((rows, u * BLK, LANES), lambda i: (0, i, 0)),
            pl.BlockSpec((rows + 2, u * BLK, 3 * LANES), lambda i: (0, i, 0)),
            whole(start.shape),
        ]
        + [whole(e.shape) for e in extra],
        out_specs=whole(shape),
        out_shape=jax.ShapeDtypeStruct(shape, F32),
        scratch_shapes=[pltpu.VMEM((3, LANES, 3 * LANES), F32)],
        compiler_params=params(),
        cost_estimate=cost(
            2 * rows * width * 9 * LANES * LANES, rows * width * 2 * 4 * LANES
        ),
        name="middle",
    )(sg, act, start, *extra)


def add_pixels(moved, taps, fpre, binput, weight, direct, total):
    acc = None
    for a in range(3):
        part = mm(moved[2 - a], taps[a])
        acc = part if acc is None else acc + part
    grad = jnp.where(fpre.astype(F32) > 0, acc, 0.0).astype(BF)
    total[...] += mm(jnp.transpose(grad), binput)
    return (mm_nt(grad, weight) + direct.astype(F32)).astype(BF)


def close_kernel(units, buf_in, sg, taps, fpre, binput, weight, fw_in, buf, fw):
    rows = fpre.shape[0] - 2
    pixels = rows * units * BLK
    channels = binput.shape[2]

    @pl.when(pl.program_id(0) == 0)
    def _():
        fw[...] = fw_in[...]

    inside = slice(1, 1 + rows)
    out = add_pixels(
        [sg[e : e + rows].reshape(pixels, 3 * LANES) for e in range(3)],
        taps,
        fpre[inside].reshape(pixels, LANES),
        binput[inside].reshape(pixels, channels),
        weight[...],
        buf_in[inside].reshape(pixels, channels),
        fw,
    )
    buf[inside] = out.reshape(rows, units * BLK, channels)
    for e in (0, rows + 1):
        buf[e] = buf_in[e]


def close_block(buf, sg, taps, fpre, binput, weight, fw_in, start):
    rows, _, channels = binput.shape
    width = sg.shape[1]
    blocks = width // BLK
    u = unit(blocks, start, 3)
    first = start // u
    wide = lambda c: pl.BlockSpec((rows, u * BLK, c), lambda i: (0, first + i, 0))
    pixels = rows * width
    return pl.pallas_call(
        functools.partial(close_kernel, u),
        grid=(blocks // u,),
        in_specs=[
            wide(channels),
            pl.BlockSpec((sg.shape[0], u * BLK, 3 * LANES), lambda i: (0, i, 0)),
            whole(taps.shape),
            wide(LANES),
            wide(channels),
            whole(weight.shape),
            whole(fw_in.shape),
        ],
        out_specs=[wide(channels), whole(fw_in.shape)],
        out_shape=[
            jax.ShapeDtypeStruct(buf.shape, BF),
            jax.ShapeDtypeStruct(fw_in.shape, F32),
        ],
        input_output_aliases={0: 0},
        compiler_params=params(),
        cost_estimate=cost(
            2 * pixels * LANES * (9 * LANES + 2 * channels),
            2 * pixels * (3 * channels + 4 * LANES),
        ),
        name="close_block",
    )(buf, sg, taps, hbm(fpre), hbm(binput), weight, fw_in)


def edge_kernel(buf_in, sg, taps, fpre, binput, weight, fw_in, buf, fw, total):
    step = pl.program_id(0)

    @pl.when(step == 0)
    def _():
        total[...] = fw_in[...]

    buf[0] = add_pixels(
        [sg[0, e] for e in range(3)],
        taps,
        fpre[0],
        binput[0],
        weight[...],
        buf_in[0],
        total,
    )

    @pl.when(step == pl.num_programs(0) - 1)
    def _():
        for t in range(binput.shape[2] // LANES):
            fw[t * LANES : (t + 1) * LANES, :] = jnp.transpose(
                total[:, t * LANES : (t + 1) * LANES]
            )


def close_edges(buf, sg, taps, fpre, binput, weight, fw_in):
    rows, _, channels = binput.shape
    width = sg.shape[2]
    flat = lambda c: pl.BlockSpec((1, width, c), lambda i: (i * (rows - 1), 0, 0))
    return pl.pallas_call(
        edge_kernel,
        grid=(2,),
        in_specs=[
            flat(channels),
            pl.BlockSpec((1, 3, width, 3 * LANES), lambda i: (i, 0, 0, 0)),
            whole(taps.shape),
            flat(LANES),
            flat(channels),
            whole(weight.shape),
            whole(fw_in.shape),
        ],
        out_specs=[flat(channels), whole((channels, LANES))],
        out_shape=[
            jax.ShapeDtypeStruct(buf.shape, BF),
            jax.ShapeDtypeStruct((channels, LANES), F32),
        ],
        scratch_shapes=[pltpu.VMEM(fw_in.shape, F32)],
        input_output_aliases={0: 0},
        compiler_params=params(),
        cost_estimate=cost(
            4 * width * LANES * (9 * LANES + 2 * channels), 12 * width * channels
        ),
        name="close_edges",
    )(buf, sg, taps, hbm(fpre), hbm(binput), weight, fw_in)


def exchange(value):
    return lax.all_to_all(value, AXIS, 0, 0, tiled=True)


def exchange_chips(value, count):
    same_core = [list(range(c, count, 2)) for c in range(2)]
    return lax.all_to_all(value, AXIS, 0, 0, tiled=True, axis_index_groups=same_core)


def swap_cores(value, count):
    return lax.ppermute(value, AXIS, [(i, i ^ 1) for i in range(count)])


def edges(value, count):
    up = [(i, i + 1) for i in range(count - 1)]
    down = [(i + 1, i) for i in range(count - 1)]
    return lax.ppermute(value[-1:], AXIS, up), lax.ppermute(value[:1], AXIS, down)


def sorted_taps(ext, width):
    return jnp.concatenate(beside(ext[:, : width + 2])[::-1], axis=2)


def beside(value):
    width = value.shape[1] - 2
    return [value[:, b : b + width] for b in range(3)]


def shards(
    block_input,
    first_pre,
    second_pre,
    output_pre,
    output_grad,
    first_weight,
    middle_weight,
    last_weight,
):
    tile_rows, map_cols, channels = block_input.shape
    inner = first_pre.shape[2]
    count = lax.axis_size(AXIS)
    factor = 1.0 / math.sqrt(tile_rows * map_cols * count)
    own = channels // count
    join = LANES // own
    groups = BLK // join
    blocks = map_cols // BLK
    head = 4 * (3 * blocks // 16)
    tail = blocks - head
    split = head * BLK
    closed = head - 2
    seam = closed * BLK

    turned = jnp.transpose(output_grad, (1, 2, 0)).reshape(map_cols * own, -1)
    send_a = pack(turned, count, tile_rows, groups, 0, head)
    recv_a = exchange(send_a)
    turned, first_pre, _ = lax.optimization_barrier((turned, first_pre, send_a))
    send_b = pack(turned, count, tile_rows, groups, head, tail)

    size = join * LANES
    lane = jnp.arange(size)
    src, col, chan = lane // LANES, lane % LANES // own, lane % own
    lane_sort = (
        (col * LANES + src * own + chan)[:, None] == lane[None, :]
    ).astype(BF)
    pixel = jnp.arange(tile_rows * BLK)
    row, column = pixel // BLK, pixel % BLK
    place = (column % join * groups + column // join) * tile_rows + row
    pixel_sort = (place[:, None] == pixel[None, :]).astype(BF)
    taps = jnp.transpose(middle_weight, (0, 1, 3, 2)).reshape(3, 3 * inner, inner)

    act = jnp.pad(jnp.maximum(first_pre, 0), ((1, 1), (1, 1), (0, 0)))
    act = jnp.concatenate(beside(act), axis=2)
    act_a, act_b = act[:, :split], act[:, split:]
    rim_act = jnp.concatenate([act[1:2], act[-2:-1]], axis=0)
    lw0 = jnp.zeros((channels // LANES, inner, LANES), F32)
    mw0 = jnp.zeros((3, inner, 3 * inner), F32)
    fw0 = jnp.zeros((inner, channels), F32)

    (send_b, lane_sort, pixel_sort, taps, act_a, act_b, rim_act, lw0, mw0, fw0) = (
        lax.optimization_barrier(
            (send_b, lane_sort, pixel_sort, taps, act_a, act_b, rim_act, lw0, mw0, fw0)
        )
    )
    recv_b = exchange(send_b)
    sorts = (lane_sort, pixel_sort)

    buf, sg_a, lw = open_block(
        None, recv_a, output_pre, second_pre, *sorts, last_weight, lw0, join, 0
    )
    mw = middle(sg_a, act_a, mw0)
    left = jnp.pad(sg_a, ((0, 0), (1, 0), (0, 0)))
    buf, fw = close_block(
        buf,
        sorted_taps(left, seam),
        taps,
        first_pre,
        block_input,
        first_weight,
        fw0,
        0,
    )

    lw, mw, fw = lax.optimization_barrier((lw, mw, fw))
    buf, sg_b, lw = open_block(
        buf, recv_b, output_pre, second_pre, *sorts, last_weight, lw, join, head
    )
    rims = jnp.concatenate(
        [
            jnp.concatenate([sg_a[e : e + 1], sg_b[e : e + 1]], axis=1)
            for e in (0, tile_rows - 1)
        ],
        axis=0,
    )
    before, after = edges(rims, count)
    both = middle(
        sg_b, act_b, mw, lw, jnp.concatenate([before, after], axis=0), rim_act
    )

    odd = lax.axis_index(AXIS) % 2 == 1
    half = both.shape[0] // 2
    size = half // (count // 2)
    pair = (both[:half], both[half:])
    kept, given = jnp.where(odd, pair[1], pair[0]), jnp.where(odd, pair[0], pair[1])
    part = (kept + swap_cores(given, count)).astype(BF).reshape(-1, size, LANES)
    part, fw, sg_b = lax.optimization_barrier((part, fw, sg_b))
    parts = exchange_chips(part, count).astype(F32)
    share = (jnp.sum(parts, axis=0) * factor).astype(BF)

    far = jnp.concatenate([sg_a[:, seam - 1 :], sg_b], axis=1)
    far = jnp.pad(far, ((0, 0), (0, 1), (0, 0)))
    buf, fw = close_block(
        buf,
        sorted_taps(far, map_cols - seam),
        taps,
        first_pre,
        block_input,
        first_weight,
        fw,
        closed,
    )
    low = jnp.concatenate([sg_a[:2], sg_b[:2]], axis=1)
    high = jnp.concatenate([sg_a[-2:], sg_b[-2:]], axis=1)
    rim = jnp.concatenate([before, low, high, after], axis=0)
    rim = sorted_taps(jnp.pad(rim, ((0, 0), (1, 1), (0, 0))), map_cols)
    buf, fw = close_edges(
        buf,
        rim.reshape(2, 3, map_cols, 3 * inner),
        taps,
        first_pre,
        block_input,
        first_weight,
        fw,
    )
    fw = fw.reshape(count // 2, 2, own, LANES)
    kept, given = jnp.where(odd, fw[:, 1], fw[:, 0]), jnp.where(odd, fw[:, 0], fw[:, 1])
    fw = (kept + swap_cores(given, count)).astype(BF)
    got = exchange_chips(
        jnp.concatenate([jnp.broadcast_to(share[None], part.shape), fw], axis=1), count
    )
    first_wgrad = jnp.sum(got[:, size:].astype(F32), axis=0) * factor
    mine = got[:, :size].reshape(half, LANES)
    other = swap_cores(mine, count)
    both = jnp.where(
        odd, jnp.concatenate([other, mine]), jnp.concatenate([mine, other])
    ).astype(F32)
    middle_wgrad = both[: 9 * inner].reshape(3, 3, inner, inner)
    last_wgrad = (
        both[9 * inner :].reshape(-1, inner, LANES).transpose(1, 0, 2).reshape(inner, channels)
    )
    return (buf, first_wgrad, middle_wgrad, last_wgrad)


def solution(mesh):
    placed = (
        P(("groups", "rows"), None, None),
        P(("groups", "rows"), None, None),
        P(("groups", "rows"), None, None),
        P(("groups", "rows"), None, None),
        P("groups", None, "rows"),
        P(),
        P(),
        P(),
    )
    return jax.shard_map(
        shards,
        mesh=mesh,
        in_specs=placed,
        out_specs=(
            P(("groups", "rows"), None, None),
            P(("groups", "rows"), None),
            P("groups", None, None, None),
            P("groups", None),
        ),
        check_vma=False,
    )
```

```python
import functools
import math

import jax
import jax.numpy as jnp
from jax import lax
from jax.experimental import pallas as pl
from jax.experimental.pallas import tpu as pltpu
from jax.sharding import PartitionSpec as P

BF = jnp.bfloat16
F32 = jnp.float32
AXIS = "rows"
BLK = 16
LANES = 128


def dims(lhs, rhs):
    return (((lhs,), (rhs,)), ((), ()))


def mm(a, b):
    return lax.dot_general(a, b, dims(1, 0), preferred_element_type=F32)


def mm_nt(a, b):
    return lax.dot_general(a, b, dims(1, 1), preferred_element_type=F32)


def unit(count, offset, cap):
    return max(u for u in range(1, cap + 1) if count % u == 0 and offset % u == 0)


def params():
    return pltpu.CompilerParams(vmem_limit_bytes=24 * 2**20)


def hbm(value):
    return pltpu.with_memory_space_constraint(value, pltpu.HBM)


def cost(flops, nbytes):
    return pl.CostEstimate(
        flops=int(flops) // 64, transcendentals=0, bytes_accessed=int(nbytes) // 64
    )


def whole(shape):
    zeros = (0,) * len(shape)
    return pl.BlockSpec(shape, lambda i: zeros)


def eye(size):
    a = lax.broadcasted_iota(jnp.int32, (size, size), 0)
    b = lax.broadcasted_iota(jnp.int32, (size, size), 1)
    return (a == b).astype(BF)


def pack_kernel(tile_rows, groups, start, x, eye_ref, out, held, ready, came, gone):
    side = eye_ref.shape[0]
    per = side // tile_rows
    steps, count, units = ready.shape[:3]
    depth = groups * LANES
    size = units * depth
    loads = [
        pltpu.make_async_copy(
            x.at[pl.ds(start * depth + k * size, size), :], held.at[k], came.at[k]
        )
        for k in range(steps)
    ]
    stores = [
        pltpu.make_async_copy(
            ready.at[k], out.at[:, pl.ds(k * units, units), :, :], gone.at[k]
        )
        for k in range(steps)
    ]
    for load in loads:
        load.start()
    for k in range(steps):
        loads[k].wait()
        for u in range(units):
            for h in range(held.shape[2] // side):
                part = held[
                    k, u * depth : (u + 1) * depth, h * side : (h + 1) * side
                ]
                turned = mm_nt(eye_ref[...], part).astype(BF)
                for g in range(groups):
                    piece = turned[:, g * LANES : (g + 1) * LANES]
                    ready[
                        k,
                        h * per : (h + 1) * per,
                        u,
                        g * tile_rows : (g + 1) * tile_rows,
                        :,
                    ] = piece.reshape(per, tile_rows, LANES)
        stores[k].start()
    for store in stores:
        store.wait()


def pack(x, count, tile_rows, groups, start, blocks):
    depth = groups * LANES
    height = x.shape[1]
    side = 256 if height % 256 == 0 else LANES
    u = unit(blocks, 0, 2)
    steps = blocks // u
    anywhere = lambda: pl.BlockSpec(memory_space=pltpu.HBM)
    return pl.pallas_call(
        functools.partial(pack_kernel, tile_rows, groups, start),
        in_specs=[anywhere(), pl.BlockSpec(memory_space=pltpu.VMEM)],
        out_specs=anywhere(),
        out_shape=pltpu.HBM((count, blocks, groups * tile_rows, LANES), BF),
        scratch_shapes=[
            pltpu.VMEM((steps, u * depth, height), BF),
            pltpu.VMEM((steps, count, u, groups * tile_rows, LANES), BF),
            pltpu.SemaphoreType.DMA((steps,)),
            pltpu.SemaphoreType.DMA((steps,)),
        ],
        compiler_params=pltpu.CompilerParams(vmem_limit_bytes=24 * 2**20),
        cost_estimate=cost(
            2 * height * side * blocks * depth, 4 * blocks * depth * height
        ),
        name="pack",
    )(hbm(x), eye(side))


def open_kernel(units, join, alias, *refs):
    if alias:
        refs = refs[1:]
    (recv, opre, spre, lanes_ref, pixels_ref, weight, lw_in, buf, sg, lw) = refs
    rows = opre.shape[0]
    tiles = recv.shape[0] // join
    height = recv.shape[2]
    pixels = rows * units * BLK

    @pl.when(pl.program_id(0) == 0)
    def _():
        lw[...] = lw_in[...]

    stack = jnp.concatenate(
        [
            jnp.concatenate([recv[t * join + s, u] for s in range(join)], axis=1)
            for u in range(units)
            for t in range(tiles)
        ],
        axis=0,
    )
    sorted_lanes = mm(stack, lanes_ref[...]).astype(BF)
    for u in range(units):
        by_pixel = jnp.concatenate(
            [
                jnp.concatenate(
                    [
                        sorted_lanes[
                            (u * tiles + t) * height : (u * tiles + t + 1) * height,
                            j * LANES : (j + 1) * LANES,
                        ]
                        for t in range(tiles)
                    ],
                    axis=1,
                )
                for j in range(join)
            ],
            axis=0,
        )
        spatial = mm(pixels_ref[...], by_pixel).reshape(rows, BLK, tiles * LANES)
        cols = slice(u * BLK, (u + 1) * BLK)
        gate = opre[:, cols, :].astype(F32) > 0
        buf[:, cols, :] = jnp.where(gate, spatial, 0.0).astype(BF)
    masked = buf[...].reshape(pixels, tiles * LANES)
    pre = spre[...].reshape(pixels, LANES).astype(F32)
    inner = mm_nt(masked, weight[...])
    sg[...] = jnp.where(pre > 0, inner, 0.0).astype(BF).reshape(sg.shape)
    act = jnp.maximum(pre, 0.0).astype(BF)
    part = mm(jnp.transpose(act), masked)
    for t in range(tiles):
        lw[t] += part[:, t * LANES : (t + 1) * LANES]


def open_block(buf, recv, opre, spre, lane_sort, pixel_sort, weight, lw_in, join, start):
    rows, _, channels = opre.shape
    count, blocks, height, _ = recv.shape
    tiles = channels // LANES
    u = unit(blocks, start, 4)
    first = start // u
    alias = buf is not None
    wide = lambda c: pl.BlockSpec((rows, u * BLK, c), lambda i: (0, first + i, 0))
    pixels = rows * BLK * blocks
    call = pl.pallas_call(
        functools.partial(open_kernel, u, join, alias),
        grid=(blocks // u,),
        in_specs=([pl.BlockSpec(memory_space=pl.ANY)] if alias else [])
        + [
            pl.BlockSpec((count, u, height, LANES), lambda i: (0, i, 0, 0)),
            wide(channels),
            wide(LANES),
            whole(lane_sort.shape),
            whole(pixel_sort.shape),
            whole(weight.shape),
            whole(lw_in.shape),
        ],
        out_specs=[
            wide(channels),
            pl.BlockSpec((rows, u * BLK, LANES), lambda i: (0, i, 0)),
            whole(lw_in.shape),
        ],
        out_shape=[
            jax.ShapeDtypeStruct(opre.shape, BF),
            jax.ShapeDtypeStruct((rows, blocks * BLK, LANES), BF),
            (jax.ShapeDtypeStruct if alias else pltpu.HBM)(lw_in.shape, F32),
        ],
        input_output_aliases={0: 0} if alias else {},
        compiler_params=params(),
        cost_estimate=cost(
            2 * pixels * channels * (512 + 256 + 256), 2 * pixels * (3 * channels + 256)
        ),
        name="open_block",
    )
    args = (recv if alias else hbm(recv),) + tuple(
        hbm(v) for v in (opre, spre, lane_sort, pixel_sort, weight, lw_in)
    )
    return call(*(((buf,) + args) if alias else args))


def middle_kernel(units, sg, act, start_ref, out):
    rows = sg.shape[0]
    pixels = rows * units * BLK

    @pl.when(pl.program_id(0) == 0)
    def _():
        out[...] = start_ref[...]

    turned = jnp.transpose(sg[...].reshape(pixels, LANES))
    for a in range(3):
        window = act[a : a + rows].reshape(pixels, 3 * LANES)
        out[a] += mm(turned, window)


def middle(sg, act, start):
    rows, width, _ = sg.shape
    blocks = width // BLK
    u = unit(blocks, 0, 4)
    return pl.pallas_call(
        functools.partial(middle_kernel, u),
        grid=(blocks // u,),
        in_specs=[
            pl.BlockSpec((rows, u * BLK, LANES), lambda i: (0, i, 0)),
            pl.BlockSpec((rows + 2, u * BLK, 3 * LANES), lambda i: (0, i, 0)),
            whole(start.shape),
        ],
        out_specs=whole(start.shape),
        out_shape=jax.ShapeDtypeStruct(start.shape, F32),
        compiler_params=params(),
        cost_estimate=cost(
            2 * rows * width * 9 * LANES * LANES, rows * width * 2 * 4 * LANES
        ),
        name="middle",
    )(sg, act, start)


def rim_kernel(mw, lw, before, after, act, out):
    sums = [mw[a] for a in range(3)]
    sums[2] += mm(jnp.transpose(before[...]), act[0])
    sums[0] += mm(jnp.transpose(after[...]), act[1])
    for a in range(3):
        for b in range(3):
            top = (3 * a + b) * LANES
            out[top : top + LANES, :] = jnp.transpose(
                sums[a][:, b * LANES : (b + 1) * LANES]
            )
    for t in range(lw.shape[0]):
        top = (9 + t) * LANES
        out[top : top + LANES, :] = lw[t]


def add_rims(mw, lw, before, after, act):
    space = pl.BlockSpec(memory_space=pltpu.VMEM)
    return pl.pallas_call(
        rim_kernel,
        in_specs=[space] * 5,
        out_specs=space,
        out_shape=jax.ShapeDtypeStruct(((9 + lw.shape[0]) * LANES, LANES), F32),
        compiler_params=params(),
        cost_estimate=cost(2**20, 2**20),
        name="add_rims",
    )(mw, lw, before, after, act)


def add_pixels(moved, taps, fpre, binput, weight, direct, total):
    acc = None
    for a in range(3):
        part = mm(moved[2 - a], taps[a])
        acc = part if acc is None else acc + part
    grad = jnp.where(fpre.astype(F32) > 0, acc, 0.0).astype(BF)
    total[...] += mm(jnp.transpose(grad), binput)
    return (mm_nt(grad, weight) + direct.astype(F32)).astype(BF)


def close_kernel(units, buf_in, sg, taps, fpre, binput, weight, fw_in, buf, fw):
    rows = fpre.shape[0] - 2
    pixels = rows * units * BLK
    channels = binput.shape[2]

    @pl.when(pl.program_id(0) == 0)
    def _():
        fw[...] = fw_in[...]

    inside = slice(1, 1 + rows)
    out = add_pixels(
        [sg[e : e + rows].reshape(pixels, 3 * LANES) for e in range(3)],
        taps,
        fpre[inside].reshape(pixels, LANES),
        binput[inside].reshape(pixels, channels),
        weight[...],
        buf_in[inside].reshape(pixels, channels),
        fw,
    )
    buf[inside] = out.reshape(rows, units * BLK, channels)
    for e in (0, rows + 1):
        buf[e] = buf_in[e]


def close_block(buf, sg, taps, fpre, binput, weight, fw_in, start):
    rows, _, channels = binput.shape
    width = sg.shape[1]
    blocks = width // BLK
    u = unit(blocks, start, 3)
    first = start // u
    wide = lambda c: pl.BlockSpec((rows, u * BLK, c), lambda i: (0, first + i, 0))
    pixels = rows * width
    return pl.pallas_call(
        functools.partial(close_kernel, u),
        grid=(blocks // u,),
        in_specs=[
            wide(channels),
            pl.BlockSpec((sg.shape[0], u * BLK, 3 * LANES), lambda i: (0, i, 0)),
            whole(taps.shape),
            wide(LANES),
            wide(channels),
            whole(weight.shape),
            whole(fw_in.shape),
        ],
        out_specs=[wide(channels), whole(fw_in.shape)],
        out_shape=[
            jax.ShapeDtypeStruct(buf.shape, BF),
            pltpu.HBM(fw_in.shape, F32),
        ],
        input_output_aliases={0: 0},
        compiler_params=params(),
        cost_estimate=cost(
            2 * pixels * LANES * (9 * LANES + 2 * channels),
            2 * pixels * (3 * channels + 4 * LANES),
        ),
        name="close_block",
    )(buf, sg, hbm(taps), hbm(fpre), hbm(binput), hbm(weight), hbm(fw_in))


def edge_kernel(buf_in, sg, taps, fpre, binput, weight, fw_in, buf, fw, total):
    step = pl.program_id(0)

    @pl.when(step == 0)
    def _():
        total[...] = fw_in[...]

    buf[0] = add_pixels(
        [sg[0, e] for e in range(3)],
        taps,
        fpre[0],
        binput[0],
        weight[...],
        buf_in[0],
        total,
    )

    @pl.when(step == pl.num_programs(0) - 1)
    def _():
        for t in range(binput.shape[2] // LANES):
            fw[t * LANES : (t + 1) * LANES, :] = jnp.transpose(
                total[:, t * LANES : (t + 1) * LANES]
            )


def close_edges(buf, sg, taps, fpre, binput, weight, fw_in):
    rows, _, channels = binput.shape
    width = sg.shape[2]
    flat = lambda c: pl.BlockSpec((1, width, c), lambda i: (i * (rows - 1), 0, 0))
    return pl.pallas_call(
        edge_kernel,
        grid=(2,),
        in_specs=[
            flat(channels),
            pl.BlockSpec((1, 3, width, 3 * LANES), lambda i: (i, 0, 0, 0)),
            whole(taps.shape),
            flat(LANES),
            flat(channels),
            whole(weight.shape),
            whole(fw_in.shape),
        ],
        out_specs=[flat(channels), whole((channels, LANES))],
        out_shape=[
            jax.ShapeDtypeStruct(buf.shape, BF),
            jax.ShapeDtypeStruct((channels, LANES), F32),
        ],
        scratch_shapes=[pltpu.VMEM(fw_in.shape, F32)],
        input_output_aliases={0: 0},
        compiler_params=params(),
        cost_estimate=cost(
            4 * width * LANES * (9 * LANES + 2 * channels), 12 * width * channels
        ),
        name="close_edges",
    )(buf, sg, hbm(taps), hbm(fpre), hbm(binput), hbm(weight), hbm(fw_in))


def finish_kernel(size, factor, odd_ref, mine, other, mw, lw, fw):
    chips = mine.shape[0]
    odd = odd_ref[0] == 1
    top = mw.shape[0]
    for h in range(2):
        for k in range(chips):
            a, b = mine[k, :size, :].astype(F32), other[k, :size, :].astype(F32)
            value = jnp.where(odd, a if h else b, b if h else a)
            start = (h * chips + k) * size
            at = start
            while at < start + size:
                stop = min(start + size, (at // LANES + 1) * LANES)
                piece = value[at - start : stop - start]
                if at < top:
                    mw[at:stop, :] = piece
                else:
                    t, m = divmod(at - top, LANES)
                    lw[m : m + stop - at, t * LANES : (t + 1) * LANES] = piece
                at = stop
    total = mine[0, size:, :].astype(F32)
    for k in range(1, chips):
        total = total + mine[k, size:, :].astype(F32)
    fw[...] = total * factor


def finish(odd, mine, other, size, factor, inner, channels):
    own = mine.shape[1] - size
    space = lambda: pl.BlockSpec(memory_space=pltpu.VMEM)
    return pl.pallas_call(
        functools.partial(finish_kernel, size, factor),
        in_specs=[pl.BlockSpec(memory_space=pltpu.SMEM), space(), space()],
        out_specs=[space(), space(), space()],
        out_shape=[
            jax.ShapeDtypeStruct((9 * inner, LANES), F32),
            jax.ShapeDtypeStruct((inner, channels), F32),
            jax.ShapeDtypeStruct((own, LANES), F32),
        ],
        compiler_params=pltpu.CompilerParams(vmem_limit_bytes=24 * 2**20),
        name="finish",
    )(odd, mine, other)


def exchange(value):
    return lax.all_to_all(value, AXIS, 0, 0, tiled=True)


def exchange_chips(value, count):
    same_core = [list(range(c, count, 2)) for c in range(2)]
    return lax.all_to_all(value, AXIS, 0, 0, tiled=True, axis_index_groups=same_core)


def swap_cores(value, count):
    return lax.ppermute(value, AXIS, [(i, i ^ 1) for i in range(count)])


def edges(first, last, count):
    odd = lax.axis_index(AXIS) % 2 == 1
    near = swap_cores(jnp.where(odd, first, last), count)
    pairs = [(i, i + 1) for i in range(1, count - 1, 2)]
    across = lax.ppermute(
        jnp.where(odd, last, first), AXIS, pairs + [(j, i) for i, j in pairs]
    )
    return jnp.where(odd, near, across), jnp.where(odd, across, near)


def sorted_taps(ext, width):
    return jnp.concatenate(beside(ext[:, : width + 2])[::-1], axis=2)


def beside(value):
    width = value.shape[1] - 2
    return [value[:, b : b + width] for b in range(3)]


def shards(
    block_input,
    first_pre,
    second_pre,
    output_pre,
    output_grad,
    first_weight,
    middle_weight,
    last_weight,
):
    tile_rows, map_cols, channels = block_input.shape
    inner = first_pre.shape[2]
    count = lax.axis_size(AXIS)
    factor = 1.0 / math.sqrt(tile_rows * map_cols * count)
    own = channels // count
    join = LANES // own
    groups = BLK // join
    blocks = map_cols // BLK
    head = 4 * (3 * blocks // 16)
    tail = blocks - head
    split = head * BLK
    closed = head - 2
    seam = closed * BLK

    turned = jnp.transpose(output_grad, (1, 2, 0)).reshape(map_cols * own, -1)
    send_a = pack(turned, count, tile_rows, groups, 0, head)
    recv_a = exchange(send_a)
    turned, first_pre, _ = lax.optimization_barrier((turned, first_pre, send_a))
    send_b = pack(turned, count, tile_rows, groups, head, tail)

    size = join * LANES
    lane = jnp.arange(size)
    src, col, chan = lane // LANES, lane % LANES // own, lane % own
    lane_sort = (
        (col * LANES + src * own + chan)[:, None] == lane[None, :]
    ).astype(BF)
    pixel = jnp.arange(tile_rows * BLK)
    row, column = pixel // BLK, pixel % BLK
    place = (column % join * groups + column // join) * tile_rows + row
    pixel_sort = (place[:, None] == pixel[None, :]).astype(BF)
    taps = jnp.transpose(middle_weight, (0, 1, 3, 2)).reshape(3, 3 * inner, inner)

    act = jnp.pad(jnp.maximum(first_pre, 0), ((1, 1), (1, 1), (0, 0)))
    act = jnp.concatenate(beside(act), axis=2)
    act_a, act_b = act[:, :split], act[:, split:]
    rim_act = jnp.concatenate([act[1:2], act[-2:-1]], axis=0)
    lw0 = jnp.zeros((channels // LANES, inner, LANES), F32)
    mw0 = jnp.zeros((3, inner, 3 * inner), F32)
    fw0 = jnp.zeros((inner, channels), F32)

    (send_b, lane_sort, pixel_sort, taps, act_a, act_b, rim_act, lw0, mw0, fw0) = (
        lax.optimization_barrier(
            (send_b, lane_sort, pixel_sort, taps, act_a, act_b, rim_act, lw0, mw0, fw0)
        )
    )
    recv_b = exchange(send_b)
    sorts = (lane_sort, pixel_sort)

    buf, sg_a, lw = open_block(
        None, recv_a, output_pre, second_pre, *sorts, last_weight, lw0, join, 0
    )
    mw = middle(sg_a, act_a, mw0)
    left = jnp.pad(sg_a, ((0, 0), (1, 0), (0, 0)))
    buf, fw = close_block(
        buf,
        sorted_taps(left, seam),
        taps,
        first_pre,
        block_input,
        first_weight,
        fw0,
        0,
    )

    lw, mw, fw = lax.optimization_barrier((lw, mw, fw))
    buf, sg_b, lw = open_block(
        buf, recv_b, output_pre, second_pre, *sorts, last_weight, lw, join, head
    )
    first, last = [
        jnp.concatenate([sg_a[e : e + 1], sg_b[e : e + 1]], axis=1)
        for e in (0, tile_rows - 1)
    ]
    before, after = edges(first, last, count)
    mw = middle(sg_b, act_b, mw)
    both = add_rims(mw, lw, before[0], after[0], rim_act)

    odd = lax.axis_index(AXIS) % 2 == 1
    half = both.shape[0] // 2
    size = half // (count // 2)
    pair = (both[:half], both[half:])
    kept, given = jnp.where(odd, pair[1], pair[0]), jnp.where(odd, pair[0], pair[1])
    part = (kept + swap_cores(given, count)).astype(BF).reshape(-1, size, LANES)
    part, fw, sg_b = lax.optimization_barrier((part, fw, sg_b))
    parts = exchange_chips(part, count).astype(F32)
    share = (jnp.sum(parts, axis=0) * factor).astype(BF)

    far = jnp.concatenate([sg_a[:, seam - 1 :], sg_b], axis=1)
    far = jnp.pad(far, ((0, 0), (0, 1), (0, 0)))
    buf, fw = close_block(
        buf,
        sorted_taps(far, map_cols - seam),
        taps,
        first_pre,
        block_input,
        first_weight,
        fw,
        closed,
    )
    low = jnp.concatenate([sg_a[:2], sg_b[:2]], axis=1)
    high = jnp.concatenate([sg_a[-2:], sg_b[-2:]], axis=1)
    rim = jnp.concatenate([before, low, high, after], axis=0)
    rim = sorted_taps(jnp.pad(rim, ((0, 0), (1, 1), (0, 0))), map_cols)
    buf, fw = close_edges(
        buf,
        rim.reshape(2, 3, map_cols, 3 * inner),
        taps,
        first_pre,
        block_input,
        first_weight,
        fw,
    )
    fw = fw.reshape(count // 2, 2, own, LANES)
    kept, given = jnp.where(odd, fw[:, 1], fw[:, 0]), jnp.where(odd, fw[:, 0], fw[:, 1])
    fw = (kept + swap_cores(given, count)).astype(BF)
    got = exchange_chips(
        jnp.concatenate([jnp.broadcast_to(share[None], part.shape), fw], axis=1), count
    )
    other = swap_cores(got, count)
    middle_wgrad, last_wgrad, first_wgrad = finish(
        odd.astype(jnp.int32).reshape(1), got, other, size, factor, inner, channels
    )
    return (buf, first_wgrad, middle_wgrad.reshape(3, 3, inner, inner), last_wgrad)


def solution(mesh):
    placed = (
        P(("groups", "rows"), None, None),
        P(("groups", "rows"), None, None),
        P(("groups", "rows"), None, None),
        P(("groups", "rows"), None, None),
        P("groups", None, "rows"),
        P(),
        P(),
        P(),
    )
    return jax.shard_map(
        shards,
        mesh=mesh,
        in_specs=placed,
        out_specs=(
            P(("groups", "rows"), None, None),
            P(("groups", "rows"), None),
            P("groups", None, None, None),
            P("groups", None),
        ),
        check_vma=False,
    )
```

```python
import functools
import math

import jax
import jax.numpy as jnp
from jax import lax
from jax.experimental import pallas as pl
from jax.experimental.pallas import tpu as pltpu
from jax.sharding import PartitionSpec as P

BF = jnp.bfloat16
F32 = jnp.float32
AXIS = "rows"
BLK = 16
LANES = 128


def dims(lhs, rhs):
    return (((lhs,), (rhs,)), ((), ()))


def mm(a, b):
    return lax.dot_general(a, b, dims(1, 0), preferred_element_type=F32)


def mm_nt(a, b):
    return lax.dot_general(a, b, dims(1, 1), preferred_element_type=F32)


def mm_tn(a, b):
    return lax.dot_general(a, b, dims(0, 0), preferred_element_type=F32)


def unit(count, cap):
    return max(u for u in range(1, cap + 1) if count % u == 0)


def params():
    return pltpu.CompilerParams(vmem_limit_bytes=24 * 2**20)


def hbm(value):
    return pltpu.with_memory_space_constraint(value, pltpu.HBM)


def cost(flops, nbytes):
    return pl.CostEstimate(
        flops=int(flops) // 64, transcendentals=0, bytes_accessed=int(nbytes) // 64
    )


def whole(shape):
    zeros = (0,) * len(shape)
    return pl.BlockSpec(shape, lambda i: zeros)


def at_columns(rows, units, channels, start):
    return pl.BlockSpec(
        (pl.Element(rows), pl.Element(units * BLK), pl.Element(channels)),
        lambda i: (0, pl.multiple_of((start + i * units) * BLK, BLK), 0),
    )


def eye(size):
    a = lax.broadcasted_iota(jnp.int32, (size, size), 0)
    b = lax.broadcasted_iota(jnp.int32, (size, size), 1)
    return (a == b).astype(BF)


def pack_kernel(tile_rows, groups, start, x, eye_ref, out, held, ready, came, gone):
    side = eye_ref.shape[0]
    per = side // tile_rows
    steps, count, units = ready.shape[:3]
    depth = groups * LANES
    size = units * depth
    loads = [
        pltpu.make_async_copy(
            x.at[pl.ds(start * depth + k * size, size), :], held.at[k], came.at[k]
        )
        for k in range(steps)
    ]
    stores = [
        pltpu.make_async_copy(
            ready.at[k], out.at[:, pl.ds(k * units, units), :, :], gone.at[k]
        )
        for k in range(steps)
    ]
    for load in loads:
        load.start()
    for k in range(steps):
        loads[k].wait()
        for u in range(units):
            for h in range(held.shape[2] // side):
                part = held[
                    k, u * depth : (u + 1) * depth, h * side : (h + 1) * side
                ]
                turned = mm_nt(eye_ref[...], part).astype(BF)
                for g in range(groups):
                    piece = turned[:, g * LANES : (g + 1) * LANES]
                    ready[
                        k,
                        h * per : (h + 1) * per,
                        u,
                        g * tile_rows : (g + 1) * tile_rows,
                        :,
                    ] = piece.reshape(per, tile_rows, LANES)
        stores[k].start()
    for store in stores:
        store.wait()


def pack(x, count, tile_rows, groups, start, blocks):
    depth = groups * LANES
    height = x.shape[1]
    side = 256 if height % 256 == 0 else LANES
    u = unit(blocks, 2)
    steps = blocks // u
    anywhere = lambda: pl.BlockSpec(memory_space=pltpu.HBM)
    return pl.pallas_call(
        functools.partial(pack_kernel, tile_rows, groups, start),
        in_specs=[anywhere(), pl.BlockSpec(memory_space=pltpu.VMEM)],
        out_specs=anywhere(),
        out_shape=pltpu.HBM((count, blocks, groups * tile_rows, LANES), BF),
        scratch_shapes=[
            pltpu.VMEM((steps, u * depth, height), BF),
            pltpu.VMEM((steps, count, u, groups * tile_rows, LANES), BF),
            pltpu.SemaphoreType.DMA((steps,)),
            pltpu.SemaphoreType.DMA((steps,)),
        ],
        compiler_params=pltpu.CompilerParams(vmem_limit_bytes=24 * 2**20),
        cost_estimate=cost(
            2 * height * side * blocks * depth, 4 * blocks * depth * height
        ),
        name="pack",
    )(hbm(x), eye(side))


def open_kernel(units, join, alias, *refs):
    if alias:
        refs = refs[1:]
    (recv, opre, spre, lanes_ref, pixels_ref, weight, lw_in, buf, sg, lw) = refs
    rows = opre.shape[0]
    tiles = recv.shape[0] // join
    height = recv.shape[2]
    pixels = rows * units * BLK

    @pl.when(pl.program_id(0) == 0)
    def _():
        lw[...] = lw_in[...]

    stack = jnp.concatenate(
        [
            jnp.concatenate([recv[t * join + s, u] for s in range(join)], axis=1)
            for u in range(units)
            for t in range(tiles)
        ],
        axis=0,
    )
    sorted_lanes = mm(stack, lanes_ref[...]).astype(BF)
    for u in range(units):
        by_pixel = jnp.concatenate(
            [
                jnp.concatenate(
                    [
                        sorted_lanes[
                            (u * tiles + t) * height : (u * tiles + t + 1) * height,
                            j * LANES : (j + 1) * LANES,
                        ]
                        for t in range(tiles)
                    ],
                    axis=1,
                )
                for j in range(join)
            ],
            axis=0,
        )
        spatial = mm(pixels_ref[...], by_pixel).reshape(rows, BLK, tiles * LANES)
        cols = slice(u * BLK, (u + 1) * BLK)
        gate = opre[:, cols, :].astype(F32) > 0
        buf[:, cols, :] = jnp.where(gate, spatial, 0.0).astype(BF)
    masked = buf[...].reshape(pixels, tiles * LANES)
    pre = spre[...].reshape(pixels, LANES).astype(F32)
    inner = mm_nt(masked, weight[...])
    sg[...] = jnp.where(pre > 0, inner, 0.0).astype(BF).reshape(sg.shape)
    act = jnp.maximum(pre, 0.0).astype(BF)
    part = mm_tn(act, masked)
    for t in range(tiles):
        lw[t] += part[:, t * LANES : (t + 1) * LANES]


def open_block(buf, recv, opre, spre, lane_sort, pixel_sort, weight, lw_in, join, start):
    rows, _, channels = opre.shape
    count, blocks, height, _ = recv.shape
    tiles = channels // LANES
    u = unit(blocks, 4)
    alias = buf is not None
    wide = lambda c: at_columns(rows, u, c, start)
    pixels = rows * BLK * blocks
    call = pl.pallas_call(
        functools.partial(open_kernel, u, join, alias),
        grid=(blocks // u,),
        in_specs=([pl.BlockSpec(memory_space=pl.ANY)] if alias else [])
        + [
            pl.BlockSpec((count, u, height, LANES), lambda i: (0, i, 0, 0)),
            wide(channels),
            wide(LANES),
            whole(lane_sort.shape),
            whole(pixel_sort.shape),
            whole(weight.shape),
            whole(lw_in.shape),
        ],
        out_specs=[
            wide(channels),
            pl.BlockSpec((rows, u * BLK, LANES), lambda i: (0, i, 0)),
            whole(lw_in.shape),
        ],
        out_shape=[
            jax.ShapeDtypeStruct(opre.shape, BF),
            jax.ShapeDtypeStruct((rows, blocks * BLK, LANES), BF),
            (jax.ShapeDtypeStruct if alias else pltpu.HBM)(lw_in.shape, F32),
        ],
        input_output_aliases={0: 0} if alias else {},
        compiler_params=params(),
        cost_estimate=cost(
            2 * pixels * channels * (512 + 256 + 256), 2 * pixels * (3 * channels + 256)
        ),
        name="open_block",
    )
    args = (recv if alias else hbm(recv),) + tuple(
        hbm(v) for v in (opre, spre, lane_sort, pixel_sort, weight, lw_in)
    )
    return call(*(((buf,) + args) if alias else args))


def middle_kernel(units, sg, act, start_ref, out):
    rows = sg.shape[0]
    pixels = rows * units * BLK

    @pl.when(pl.program_id(0) == 0)
    def _():
        out[...] = start_ref[...]

    turned = jnp.transpose(sg[...].reshape(pixels, LANES))
    for a in range(3):
        window = act[a : a + rows].reshape(pixels, 3 * LANES)
        out[a] += mm(turned, window)


def middle(sg, act, start):
    rows, width, _ = sg.shape
    blocks = width // BLK
    u = unit(blocks, 4)
    return pl.pallas_call(
        functools.partial(middle_kernel, u),
        grid=(blocks // u,),
        in_specs=[
            pl.BlockSpec((rows, u * BLK, LANES), lambda i: (0, i, 0)),
            pl.BlockSpec((rows + 2, u * BLK, 3 * LANES), lambda i: (0, i, 0)),
            whole(start.shape),
        ],
        out_specs=whole(start.shape),
        out_shape=jax.ShapeDtypeStruct(start.shape, F32),
        compiler_params=params(),
        cost_estimate=cost(
            2 * rows * width * 9 * LANES * LANES, rows * width * 2 * 4 * LANES
        ),
        name="middle",
    )(sg, act, start)


def rim_kernel(mw, lw, before, after, act, out):
    sums = [mw[a] for a in range(3)]
    sums[2] += mm(jnp.transpose(before[...]), act[0])
    sums[0] += mm(jnp.transpose(after[...]), act[1])
    for a in range(3):
        for b in range(3):
            top = (3 * a + b) * LANES
            out[top : top + LANES, :] = jnp.transpose(
                sums[a][:, b * LANES : (b + 1) * LANES]
            ).astype(BF)
    for t in range(lw.shape[0]):
        top = (9 + t) * LANES
        out[top : top + LANES, :] = lw[t].astype(BF)


def add_rims(mw, lw, before, after, act):
    space = pl.BlockSpec(memory_space=pltpu.VMEM)
    return pl.pallas_call(
        rim_kernel,
        in_specs=[space] * 5,
        out_specs=space,
        out_shape=jax.ShapeDtypeStruct(((9 + lw.shape[0]) * LANES, LANES), BF),
        compiler_params=params(),
        cost_estimate=cost(2**20, 2**20),
        name="add_rims",
    )(mw, lw, before, after, act)


def add_pixels(moved, taps, fpre, binput, weight, direct, total):
    acc = None
    for a in range(3):
        part = mm(moved[2 - a], taps[a])
        acc = part if acc is None else acc + part
    grad = jnp.where(fpre.astype(F32) > 0, acc, 0.0).astype(BF)
    total[...] += mm_tn(grad, binput)
    return (mm_nt(grad, weight) + direct.astype(F32)).astype(BF)


def close_kernel(units, buf_in, sg, taps, fpre, binput, weight, fw_in, buf, fw):
    rows = fpre.shape[0] - 2
    pixels = rows * units * BLK
    channels = binput.shape[2]

    @pl.when(pl.program_id(0) == 0)
    def _():
        fw[...] = fw_in[...]

    inside = slice(1, 1 + rows)
    width = units * BLK
    cols = pl.ds(pl.multiple_of(pl.program_id(0) * width, width), width)
    out = add_pixels(
        [sg[e : e + rows, cols, :].reshape(pixels, 3 * LANES) for e in range(3)],
        taps,
        fpre[inside].reshape(pixels, LANES),
        binput[inside].reshape(pixels, channels),
        weight[...],
        buf_in[inside].reshape(pixels, channels),
        fw,
    )
    buf[inside] = out.reshape(rows, units * BLK, channels)
    for e in (0, rows + 1):
        buf[e] = buf_in[e]


def close_block(buf, sg, taps, fpre, binput, weight, fw_in, start):
    rows, _, channels = binput.shape
    width = sg.shape[1]
    blocks = width // BLK
    u = unit(blocks, 4)
    wide = lambda c: at_columns(rows, u, c, start)
    pixels = rows * width
    return pl.pallas_call(
        functools.partial(close_kernel, u),
        grid=(blocks // u,),
        in_specs=[
            wide(channels),
            pl.BlockSpec(memory_space=pltpu.VMEM),
            whole(taps.shape),
            wide(LANES),
            wide(channels),
            whole(weight.shape),
            whole(fw_in.shape),
        ],
        out_specs=[wide(channels), whole(fw_in.shape)],
        out_shape=[
            jax.ShapeDtypeStruct(buf.shape, BF),
            pltpu.HBM(fw_in.shape, F32),
        ],
        input_output_aliases={0: 0},
        compiler_params=params(),
        cost_estimate=cost(
            2 * pixels * LANES * (9 * LANES + 2 * channels),
            2 * pixels * (3 * channels + 4 * LANES),
        ),
        name="close_block",
    )(buf, sg, hbm(taps), hbm(fpre), hbm(binput), hbm(weight), hbm(fw_in))


def edge_kernel(buf_in, sg, taps, fpre, binput, weight, fw_in, buf, fw, total):
    step = pl.program_id(0)

    @pl.when(step == 0)
    def _():
        total[...] = fw_in[...]

    buf[0] = add_pixels(
        [sg[step, e] for e in range(3)],
        taps,
        fpre[0],
        binput[0],
        weight[...],
        buf_in[0],
        total,
    )

    @pl.when(step == pl.num_programs(0) - 1)
    def _():
        for t in range(binput.shape[2] // LANES):
            fw[t * LANES : (t + 1) * LANES, :] = jnp.transpose(
                total[:, t * LANES : (t + 1) * LANES]
            ).astype(BF)


def close_edges(buf, sg, taps, fpre, binput, weight, fw_in):
    rows, _, channels = binput.shape
    width = sg.shape[2]
    flat = lambda c: pl.BlockSpec((1, width, c), lambda i: (i * (rows - 1), 0, 0))
    return pl.pallas_call(
        edge_kernel,
        grid=(2,),
        in_specs=[
            flat(channels),
            pl.BlockSpec(memory_space=pltpu.VMEM),
            whole(taps.shape),
            flat(LANES),
            flat(channels),
            whole(weight.shape),
            whole(fw_in.shape),
        ],
        out_specs=[flat(channels), whole((channels, LANES))],
        out_shape=[
            jax.ShapeDtypeStruct(buf.shape, BF),
            jax.ShapeDtypeStruct((channels, LANES), BF),
        ],
        scratch_shapes=[pltpu.VMEM(fw_in.shape, F32)],
        input_output_aliases={0: 0},
        compiler_params=params(),
        cost_estimate=cost(
            4 * width * LANES * (9 * LANES + 2 * channels), 12 * width * channels
        ),
        name="close_edges",
    )(buf, sg, hbm(taps), hbm(fpre), hbm(binput), hbm(weight), hbm(fw_in))


def finish_kernel(size, factor, odd_ref, mine, other, mw, lw, fw):
    chips = mine.shape[0]
    odd = odd_ref[0] == 1
    top = mw.shape[0]
    for h in range(2):
        for k in range(chips):
            a, b = mine[k, :size, :].astype(F32), other[k, :size, :].astype(F32)
            value = jnp.where(odd, a if h else b, b if h else a)
            start = (2 * k + h) * size
            at = start
            while at < start + size:
                stop = min(start + size, (at // LANES + 1) * LANES)
                piece = value[at - start : stop - start]
                if at < top:
                    mw[at:stop, :] = piece
                else:
                    t, m = divmod(at - top, LANES)
                    lw[m : m + stop - at, t * LANES : (t + 1) * LANES] = piece
                at = stop
    own = fw.shape[0]
    sums = []
    for c in range(2):
        rows = slice(size + c * own, size + (c + 1) * own)
        total = mine[0, rows, :].astype(F32) + other[0, rows, :].astype(F32)
        for k in range(1, chips):
            total += mine[k, rows, :].astype(F32) + other[k, rows, :].astype(F32)
        sums.append(total)
    fw[...] = jnp.where(odd, sums[1], sums[0]) * factor


def finish(odd, mine, other, size, factor, inner, channels):
    own = (mine.shape[1] - size) // 2
    space = lambda: pl.BlockSpec(memory_space=pltpu.VMEM)
    return pl.pallas_call(
        functools.partial(finish_kernel, size, factor),
        in_specs=[pl.BlockSpec(memory_space=pltpu.SMEM), space(), space()],
        out_specs=[space(), space(), space()],
        out_shape=[
            jax.ShapeDtypeStruct((9 * inner, LANES), F32),
            jax.ShapeDtypeStruct((inner, channels), F32),
            jax.ShapeDtypeStruct((own, LANES), F32),
        ],
        compiler_params=pltpu.CompilerParams(vmem_limit_bytes=24 * 2**20),
        name="finish",
    )(odd, mine, other)


def exchange(value):
    return lax.all_to_all(value, AXIS, 0, 0, tiled=True)


def exchange_chips(value, count):
    same_core = [list(range(c, count, 2)) for c in range(2)]
    return lax.all_to_all(value, AXIS, 0, 0, tiled=True, axis_index_groups=same_core)


def swap_cores(value, count):
    return lax.ppermute(value, AXIS, [(i, i ^ 1) for i in range(count)])


def edges(first, last, count):
    odd = lax.axis_index(AXIS) % 2 == 1
    near = swap_cores(jnp.where(odd, first, last), count)
    pairs = [(i, i + 1) for i in range(1, count - 1, 2)]
    across = lax.ppermute(
        jnp.where(odd, last, first), AXIS, pairs + [(j, i) for i, j in pairs]
    )
    return jnp.where(odd, near, across), jnp.where(odd, across, near)


def sorted_taps(ext, width):
    return jnp.concatenate(beside(ext[:, : width + 2])[::-1], axis=2)


def beside(value):
    width = value.shape[1] - 2
    return [value[:, b : b + width] for b in range(3)]


def shards(
    block_input,
    first_pre,
    second_pre,
    output_pre,
    output_grad,
    first_weight,
    middle_weight,
    last_weight,
):
    tile_rows, map_cols, channels = block_input.shape
    inner = first_pre.shape[2]
    count = lax.axis_size(AXIS)
    factor = 1.0 / math.sqrt(tile_rows * map_cols * count)
    own = channels // count
    join = LANES // own
    groups = BLK // join
    blocks = map_cols // BLK
    head = 4 * (3 * blocks // 16)
    tail = blocks - head
    split = head * BLK
    closed = head - 2
    seam = closed * BLK

    turned = jnp.transpose(output_grad, (1, 2, 0)).reshape(map_cols * own, -1)
    send_a = pack(turned, count, tile_rows, groups, 0, head)
    recv_a = exchange(send_a)
    turned, first_pre, _ = lax.optimization_barrier((turned, first_pre, send_a))
    send_b = pack(turned, count, tile_rows, groups, head, tail)

    size = join * LANES
    lane = jnp.arange(size)
    src, col, chan = lane // LANES, lane % LANES // own, lane % own
    lane_sort = (
        (col * LANES + src * own + chan)[:, None] == lane[None, :]
    ).astype(BF)
    pixel = jnp.arange(tile_rows * BLK)
    row, column = pixel // BLK, pixel % BLK
    place = (column % join * groups + column // join) * tile_rows + row
    pixel_sort = (place[:, None] == pixel[None, :]).astype(BF)
    taps = jnp.transpose(middle_weight, (0, 1, 3, 2)).reshape(3, 3 * inner, inner)

    act = jnp.pad(jnp.maximum(first_pre, 0), ((1, 1), (1, 1), (0, 0)))
    act = jnp.concatenate(beside(act), axis=2)
    act_a, act_b = act[:, :split], act[:, split:]
    rim_act = jnp.concatenate([act[1:2], act[-2:-1]], axis=0)
    lw0 = jnp.zeros((channels // LANES, inner, LANES), F32)
    mw0 = jnp.zeros((3, inner, 3 * inner), F32)
    fw0 = jnp.zeros((inner, channels), F32)

    (send_b, lane_sort, pixel_sort, taps, act_a, act_b, rim_act, lw0, mw0, fw0) = (
        lax.optimization_barrier(
            (send_b, lane_sort, pixel_sort, taps, act_a, act_b, rim_act, lw0, mw0, fw0)
        )
    )
    recv_b = exchange(send_b)
    sorts = (lane_sort, pixel_sort)

    buf, sg_a, lw = open_block(
        None, recv_a, output_pre, second_pre, *sorts, last_weight, lw0, join, 0
    )
    mw = middle(sg_a, act_a, mw0)
    left = jnp.pad(sg_a, ((0, 0), (1, 0), (0, 0)))
    buf, fw = close_block(
        buf,
        sorted_taps(left, seam),
        taps,
        first_pre,
        block_input,
        first_weight,
        fw0,
        0,
    )

    lw, mw, fw = lax.optimization_barrier((lw, mw, fw))
    buf, sg_b, lw = open_block(
        buf, recv_b, output_pre, second_pre, *sorts, last_weight, lw, join, head
    )
    first, last = [
        jnp.concatenate([sg_a[e : e + 1], sg_b[e : e + 1]], axis=1)
        for e in (0, tile_rows - 1)
    ]
    before, after = edges(first, last, count)
    mw = middle(sg_b, act_b, mw)
    both = add_rims(mw, lw, before[0], after[0], rim_act)

    size = both.shape[0] // count
    part, fw, sg_b = lax.optimization_barrier(
        (both.reshape(count, size, LANES), fw, sg_b)
    )
    parts = exchange(part).astype(F32)
    share = (jnp.sum(parts, axis=0) * factor).astype(BF)

    far = jnp.concatenate([sg_a[:, seam - 1 :], sg_b], axis=1)
    far = jnp.pad(far, ((0, 0), (0, 1), (0, 0)))
    buf, fw = close_block(
        buf,
        sorted_taps(far, map_cols - seam),
        taps,
        first_pre,
        block_input,
        first_weight,
        fw,
        closed,
    )
    low = jnp.concatenate([sg_a[:2], sg_b[:2]], axis=1)
    high = jnp.concatenate([sg_a[-2:], sg_b[-2:]], axis=1)
    rim = jnp.concatenate([before, low, high, after], axis=0)
    rim = sorted_taps(jnp.pad(rim, ((0, 0), (1, 1), (0, 0))), map_cols)
    buf, fw = close_edges(
        buf,
        rim.reshape(2, 3, map_cols, 3 * inner),
        taps,
        first_pre,
        block_input,
        first_weight,
        fw,
    )
    chips = count // 2
    got = exchange_chips(
        jnp.concatenate(
            [
                jnp.broadcast_to(share[None], (chips, size, LANES)),
                fw.reshape(chips, 2 * own, LANES),
            ],
            axis=1,
        ),
        count,
    )
    other = swap_cores(got, count)
    middle_wgrad, last_wgrad, first_wgrad = finish(
        (lax.axis_index(AXIS) % 2).reshape(1), got, other, size, factor, inner, channels
    )
    return (buf, first_wgrad, middle_wgrad.reshape(3, 3, inner, inner), last_wgrad)


def solution(mesh):
    placed = (
        P(("groups", "rows"), None, None),
        P(("groups", "rows"), None, None),
        P(("groups", "rows"), None, None),
        P(("groups", "rows"), None, None),
        P("groups", None, "rows"),
        P(),
        P(),
        P(),
    )
    return jax.shard_map(
        shards,
        mesh=mesh,
        in_specs=placed,
        out_specs=(
            P(("groups", "rows"), None, None),
            P(("groups", "rows"), None),
            P("groups", None, None, None),
            P("groups", None),
        ),
        check_vma=False,
    )
```

```python
import functools
import math

import jax
import jax.numpy as jnp
from jax import lax
from jax.experimental import pallas as pl
from jax.experimental.pallas import tpu as pltpu
from jax.sharding import PartitionSpec as P

BF = jnp.bfloat16
F32 = jnp.float32
AXIS = "rows"
BLK = 16
LANES = 128


def dims(lhs, rhs):
    return (((lhs,), (rhs,)), ((), ()))


def mm(a, b):
    return lax.dot_general(a, b, dims(1, 0), preferred_element_type=F32)


def mm_nt(a, b):
    return lax.dot_general(a, b, dims(1, 1), preferred_element_type=F32)


def mm_tn(a, b):
    return lax.dot_general(a, b, dims(0, 0), preferred_element_type=F32)


def unit(count, cap):
    return max(u for u in range(1, cap + 1) if count % u == 0)


def params():
    return pltpu.CompilerParams(vmem_limit_bytes=32 * 2**20)


def hbm(value):
    return pltpu.with_memory_space_constraint(value, pltpu.HBM)


def cost(flops, nbytes):
    return pl.CostEstimate(
        flops=int(flops) // 64, transcendentals=0, bytes_accessed=int(nbytes) // 64
    )


def whole(shape):
    zeros = (0,) * len(shape)
    return pl.BlockSpec(shape, lambda i: zeros)


def at_columns(rows, units, channels, start):
    return pl.BlockSpec(
        (pl.Element(rows), pl.Element(units * BLK), pl.Element(channels)),
        lambda i: (0, pl.multiple_of((start + i * units) * BLK, BLK), 0),
    )


def eye(size):
    a = lax.broadcasted_iota(jnp.int32, (size, size), 0)
    b = lax.broadcasted_iota(jnp.int32, (size, size), 1)
    return (a == b).astype(BF)


def pack_kernel(tile_rows, groups, start, x, eye_ref, out, held, ready, came, gone):
    side = eye_ref.shape[0]
    per = side // tile_rows
    steps, count, units = ready.shape[:3]
    depth = groups * LANES
    size = units * depth
    loads = [
        pltpu.make_async_copy(
            x.at[pl.ds(start * depth + k * size, size), :], held.at[k], came.at[k]
        )
        for k in range(steps)
    ]
    stores = [
        pltpu.make_async_copy(
            ready.at[k], out.at[:, pl.ds(k * units, units), :, :], gone.at[k]
        )
        for k in range(steps)
    ]
    for load in loads:
        load.start()
    for k in range(steps):
        loads[k].wait()
        for u in range(units):
            for h in range(held.shape[2] // side):
                part = held[
                    k, u * depth : (u + 1) * depth, h * side : (h + 1) * side
                ]
                turned = mm_nt(eye_ref[...], part).astype(BF)
                for g in range(groups):
                    piece = turned[:, g * LANES : (g + 1) * LANES]
                    ready[
                        k,
                        h * per : (h + 1) * per,
                        u,
                        g * tile_rows : (g + 1) * tile_rows,
                        :,
                    ] = piece.reshape(per, tile_rows, LANES)
        stores[k].start()
    for store in stores:
        store.wait()


def pack(x, count, tile_rows, groups, start, blocks):
    depth = groups * LANES
    height = x.shape[1]
    side = 256 if height % 256 == 0 else LANES
    u = unit(blocks, 4)
    steps = blocks // u
    anywhere = lambda: pl.BlockSpec(memory_space=pltpu.HBM)
    return pl.pallas_call(
        functools.partial(pack_kernel, tile_rows, groups, start),
        in_specs=[anywhere(), pl.BlockSpec(memory_space=pltpu.VMEM)],
        out_specs=anywhere(),
        out_shape=pltpu.HBM((count, blocks, groups * tile_rows, LANES), BF),
        scratch_shapes=[
            pltpu.VMEM((steps, u * depth, height), BF),
            pltpu.VMEM((steps, count, u, groups * tile_rows, LANES), BF),
            pltpu.SemaphoreType.DMA((steps,)),
            pltpu.SemaphoreType.DMA((steps,)),
        ],
        compiler_params=pltpu.CompilerParams(vmem_limit_bytes=24 * 2**20),
        cost_estimate=cost(
            2 * height * side * blocks * depth, 4 * blocks * depth * height
        ),
        name="pack",
    )(hbm(x), eye(side))


def open_kernel(units, join, alias, *refs):
    if alias:
        refs = refs[1:]
    (recv, opre, spre, lanes_ref, pixels_ref, weight, lw_in, buf, sg, lw) = refs
    rows = opre.shape[0]
    tiles = recv.shape[0] // join
    height = recv.shape[2]
    pixels = rows * units * BLK

    @pl.when(pl.program_id(0) == 0)
    def _():
        lw[...] = lw_in[...]

    stack = jnp.concatenate(
        [
            jnp.concatenate([recv[t * join + s, u] for s in range(join)], axis=1)
            for u in range(units)
            for t in range(tiles)
        ],
        axis=0,
    )
    sorted_lanes = mm(stack, lanes_ref[...]).astype(BF)
    for u in range(units):
        by_pixel = jnp.concatenate(
            [
                jnp.concatenate(
                    [
                        sorted_lanes[
                            (u * tiles + t) * height : (u * tiles + t + 1) * height,
                            j * LANES : (j + 1) * LANES,
                        ]
                        for t in range(tiles)
                    ],
                    axis=1,
                )
                for j in range(join)
            ],
            axis=0,
        )
        spatial = mm(pixels_ref[...], by_pixel).reshape(rows, BLK, tiles * LANES)
        cols = slice(u * BLK, (u + 1) * BLK)
        gate = opre[:, cols, :].astype(F32) > 0
        buf[:, cols, :] = jnp.where(gate, spatial, 0.0).astype(BF)
    masked = buf[...].reshape(pixels, tiles * LANES)
    pre = spre[...].reshape(pixels, LANES).astype(F32)
    inner = mm_nt(masked, weight[...])
    sg[...] = jnp.where(pre > 0, inner, 0.0).astype(BF).reshape(sg.shape)
    act = jnp.maximum(pre, 0.0).astype(BF)
    part = mm_tn(act, masked)
    for t in range(tiles):
        lw[t] += part[:, t * LANES : (t + 1) * LANES]


def open_block(buf, recv, opre, spre, lane_sort, pixel_sort, weight, lw_in, join, start):
    rows, _, channels = opre.shape
    count, blocks, height, _ = recv.shape
    tiles = channels // LANES
    u = unit(blocks, 6)
    alias = buf is not None
    wide = lambda c: at_columns(rows, u, c, start)
    pixels = rows * BLK * blocks
    call = pl.pallas_call(
        functools.partial(open_kernel, u, join, alias),
        grid=(blocks // u,),
        in_specs=([pl.BlockSpec(memory_space=pl.ANY)] if alias else [])
        + [
            pl.BlockSpec((count, u, height, LANES), lambda i: (0, i, 0, 0)),
            wide(channels),
            wide(LANES),
            whole(lane_sort.shape),
            whole(pixel_sort.shape),
            whole(weight.shape),
            whole(lw_in.shape),
        ],
        out_specs=[
            wide(channels),
            pl.BlockSpec((rows, u * BLK, LANES), lambda i: (0, i, 0)),
            whole(lw_in.shape),
        ],
        out_shape=[
            jax.ShapeDtypeStruct(opre.shape, BF),
            jax.ShapeDtypeStruct((rows, blocks * BLK, LANES), BF),
            (jax.ShapeDtypeStruct if alias else pltpu.HBM)(lw_in.shape, F32),
        ],
        input_output_aliases={0: 0} if alias else {},
        compiler_params=params(),
        cost_estimate=cost(
            2 * pixels * channels * (512 + 256 + 256), 2 * pixels * (3 * channels + 256)
        ),
        name="open_block",
    )
    args = (recv if alias else hbm(recv),) + tuple(
        hbm(v) for v in (opre, spre, lane_sort, pixel_sort, weight, lw_in)
    )
    return call(*(((buf,) + args) if alias else args))


def middle_kernel(units, sg, act, start_ref, out):
    rows = sg.shape[0]
    pixels = rows * units * BLK

    @pl.when(pl.program_id(0) == 0)
    def _():
        out[...] = start_ref[...]

    turned = jnp.transpose(sg[...].reshape(pixels, LANES))
    for a in range(3):
        window = act[a : a + rows].reshape(pixels, 3 * LANES)
        out[a] += mm(turned, window)


def middle(sg, act, start):
    rows, width, _ = sg.shape
    blocks = width // BLK
    u = unit(blocks, 4)
    return pl.pallas_call(
        functools.partial(middle_kernel, u),
        grid=(blocks // u,),
        in_specs=[
            pl.BlockSpec((rows, u * BLK, LANES), lambda i: (0, i, 0)),
            pl.BlockSpec((rows + 2, u * BLK, 3 * LANES), lambda i: (0, i, 0)),
            whole(start.shape),
        ],
        out_specs=whole(start.shape),
        out_shape=jax.ShapeDtypeStruct(start.shape, F32),
        compiler_params=params(),
        cost_estimate=cost(
            2 * rows * width * 9 * LANES * LANES, rows * width * 2 * 4 * LANES
        ),
        name="middle",
    )(sg, act, start)


def rim_kernel(mw, lw, before, after, act, out):
    sums = [mw[a] for a in range(3)]
    sums[2] += mm(jnp.transpose(before[...]), act[0])
    sums[0] += mm(jnp.transpose(after[...]), act[1])
    for a in range(3):
        for b in range(3):
            top = (3 * a + b) * LANES
            out[top : top + LANES, :] = jnp.transpose(
                sums[a][:, b * LANES : (b + 1) * LANES]
            ).astype(BF)
    for t in range(lw.shape[0]):
        top = (9 + t) * LANES
        out[top : top + LANES, :] = lw[t].astype(BF)


def add_rims(mw, lw, before, after, act):
    space = pl.BlockSpec(memory_space=pltpu.VMEM)
    return pl.pallas_call(
        rim_kernel,
        in_specs=[space] * 5,
        out_specs=space,
        out_shape=jax.ShapeDtypeStruct(((9 + lw.shape[0]) * LANES, LANES), BF),
        compiler_params=params(),
        cost_estimate=cost(2**20, 2**20),
        name="add_rims",
    )(mw, lw, before, after, act)


def add_pixels(moved, taps, fpre, binput, weight, direct, total):
    acc = None
    for a in range(3):
        part = mm(moved[2 - a], taps[a])
        acc = part if acc is None else acc + part
    grad = jnp.where(fpre.astype(F32) > 0, acc, 0.0).astype(BF)
    total[...] += mm_tn(grad, binput)
    return (mm_nt(grad, weight) + direct.astype(F32)).astype(BF)


def close_kernel(units, buf_in, sg, taps, fpre, binput, weight, fw_in, buf, fw):
    rows = fpre.shape[0] - 2
    pixels = rows * units * BLK
    channels = binput.shape[2]

    @pl.when(pl.program_id(0) == 0)
    def _():
        fw[...] = fw_in[...]

    inside = slice(1, 1 + rows)
    width = units * BLK
    cols = pl.ds(pl.multiple_of(pl.program_id(0) * width, width), width)
    out = add_pixels(
        [sg[e : e + rows, cols, :].reshape(pixels, 3 * LANES) for e in range(3)],
        taps,
        fpre[inside].reshape(pixels, LANES),
        binput[inside].reshape(pixels, channels),
        weight[...],
        buf_in[inside].reshape(pixels, channels),
        fw,
    )
    buf[inside] = out.reshape(rows, units * BLK, channels)
    for e in (0, rows + 1):
        buf[e] = buf_in[e]


def close_block(buf, sg, taps, fpre, binput, weight, fw_in, start):
    rows, _, channels = binput.shape
    width = sg.shape[1]
    blocks = width // BLK
    u = unit(blocks, 7)
    wide = lambda c: at_columns(rows, u, c, start)
    pixels = rows * width
    return pl.pallas_call(
        functools.partial(close_kernel, u),
        grid=(blocks // u,),
        in_specs=[
            wide(channels),
            pl.BlockSpec(memory_space=pltpu.VMEM),
            whole(taps.shape),
            wide(LANES),
            wide(channels),
            whole(weight.shape),
            whole(fw_in.shape),
        ],
        out_specs=[wide(channels), whole(fw_in.shape)],
        out_shape=[
            jax.ShapeDtypeStruct(buf.shape, BF),
            pltpu.HBM(fw_in.shape, F32),
        ],
        input_output_aliases={0: 0},
        compiler_params=params(),
        cost_estimate=cost(
            2 * pixels * LANES * (9 * LANES + 2 * channels),
            2 * pixels * (3 * channels + 4 * LANES),
        ),
        name="close_block",
    )(buf, sg, hbm(taps), hbm(fpre), hbm(binput), hbm(weight), hbm(fw_in))


def edge_kernel(buf_in, sg, taps, fpre, binput, weight, fw_in, buf, fw, total):
    step = pl.program_id(0)

    @pl.when(step == 0)
    def _():
        total[...] = fw_in[...]

    buf[0] = add_pixels(
        [sg[step, e] for e in range(3)],
        taps,
        fpre[0],
        binput[0],
        weight[...],
        buf_in[0],
        total,
    )

    @pl.when(step == pl.num_programs(0) - 1)
    def _():
        for t in range(binput.shape[2] // LANES):
            fw[t * LANES : (t + 1) * LANES, :] = jnp.transpose(
                total[:, t * LANES : (t + 1) * LANES]
            ).astype(BF)


def close_edges(buf, sg, taps, fpre, binput, weight, fw_in):
    rows, _, channels = binput.shape
    width = sg.shape[2]
    flat = lambda c: pl.BlockSpec((1, width, c), lambda i: (i * (rows - 1), 0, 0))
    return pl.pallas_call(
        edge_kernel,
        grid=(2,),
        in_specs=[
            flat(channels),
            pl.BlockSpec(memory_space=pltpu.VMEM),
            whole(taps.shape),
            flat(LANES),
            flat(channels),
            whole(weight.shape),
            whole(fw_in.shape),
        ],
        out_specs=[flat(channels), whole((channels, LANES))],
        out_shape=[
            jax.ShapeDtypeStruct(buf.shape, BF),
            jax.ShapeDtypeStruct((channels, LANES), BF),
        ],
        scratch_shapes=[pltpu.VMEM(fw_in.shape, F32)],
        input_output_aliases={0: 0},
        compiler_params=params(),
        cost_estimate=cost(
            4 * width * LANES * (9 * LANES + 2 * channels), 12 * width * channels
        ),
        name="close_edges",
    )(buf, sg, hbm(taps), hbm(fpre), hbm(binput), hbm(weight), hbm(fw_in))


def finish_kernel(size, factor, odd_ref, mine, other, mw, lw, fw):
    chips = mine.shape[0]
    odd = odd_ref[0] == 1
    top = mw.shape[0]
    for h in range(2):
        for k in range(chips):
            a, b = mine[k, :size, :].astype(F32), other[k, :size, :].astype(F32)
            value = jnp.where(odd, a if h else b, b if h else a)
            start = (2 * k + h) * size
            at = start
            while at < start + size:
                stop = min(start + size, (at // LANES + 1) * LANES)
                piece = value[at - start : stop - start]
                if at < top:
                    mw[at:stop, :] = piece
                else:
                    t, m = divmod(at - top, LANES)
                    lw[m : m + stop - at, t * LANES : (t + 1) * LANES] = piece
                at = stop
    own = fw.shape[0]
    sums = []
    for c in range(2):
        rows = slice(size + c * own, size + (c + 1) * own)
        total = mine[0, rows, :].astype(F32) + other[0, rows, :].astype(F32)
        for k in range(1, chips):
            total += mine[k, rows, :].astype(F32) + other[k, rows, :].astype(F32)
        sums.append(total)
    fw[...] = jnp.where(odd, sums[1], sums[0]) * factor


def finish(odd, mine, other, size, factor, inner, channels):
    own = (mine.shape[1] - size) // 2
    space = lambda: pl.BlockSpec(memory_space=pltpu.VMEM)
    return pl.pallas_call(
        functools.partial(finish_kernel, size, factor),
        in_specs=[pl.BlockSpec(memory_space=pltpu.SMEM), space(), space()],
        out_specs=[space(), space(), space()],
        out_shape=[
            jax.ShapeDtypeStruct((9 * inner, LANES), F32),
            jax.ShapeDtypeStruct((inner, channels), F32),
            jax.ShapeDtypeStruct((own, LANES), F32),
        ],
        compiler_params=pltpu.CompilerParams(vmem_limit_bytes=24 * 2**20),
        name="finish",
    )(odd, mine, other)


def exchange(value):
    return lax.all_to_all(value, AXIS, 0, 0, tiled=True)


def exchange_chips(value, count):
    same_core = [list(range(c, count, 2)) for c in range(2)]
    return lax.all_to_all(value, AXIS, 0, 0, tiled=True, axis_index_groups=same_core)


def swap_cores(value, count):
    return lax.ppermute(value, AXIS, [(i, i ^ 1) for i in range(count)])


def edges(first, last, count):
    odd = lax.axis_index(AXIS) % 2 == 1
    near = swap_cores(jnp.where(odd, first, last), count)
    pairs = [(i, i + 1) for i in range(1, count - 1, 2)]
    across = lax.ppermute(
        jnp.where(odd, last, first), AXIS, pairs + [(j, i) for i, j in pairs]
    )
    return jnp.where(odd, near, across), jnp.where(odd, across, near)


def sorted_taps(ext, width):
    return jnp.concatenate(beside(ext[:, : width + 2])[::-1], axis=2)


def beside(value):
    width = value.shape[1] - 2
    return [value[:, b : b + width] for b in range(3)]


def shards(
    block_input,
    first_pre,
    second_pre,
    output_pre,
    output_grad,
    first_weight,
    middle_weight,
    last_weight,
):
    tile_rows, map_cols, channels = block_input.shape
    inner = first_pre.shape[2]
    count = lax.axis_size(AXIS)
    factor = 1.0 / math.sqrt(tile_rows * map_cols * count)
    own = channels // count
    join = LANES // own
    groups = BLK // join
    blocks = map_cols // BLK
    head = blocks - 4
    tail = blocks - head
    split = head * BLK
    closed = head - 4
    seam = closed * BLK

    turned = jnp.transpose(output_grad, (1, 2, 0)).reshape(map_cols * own, -1)
    send_a = pack(turned, count, tile_rows, groups, 0, head)
    recv_a = exchange(send_a)
    turned, first_pre, _ = lax.optimization_barrier((turned, first_pre, send_a))
    send_b = pack(turned, count, tile_rows, groups, head, tail)

    size = join * LANES
    lane = jnp.arange(size)
    src, col, chan = lane // LANES, lane % LANES // own, lane % own
    lane_sort = (
        (col * LANES + src * own + chan)[:, None] == lane[None, :]
    ).astype(BF)
    pixel = jnp.arange(tile_rows * BLK)
    row, column = pixel // BLK, pixel % BLK
    place = (column % join * groups + column // join) * tile_rows + row
    pixel_sort = (place[:, None] == pixel[None, :]).astype(BF)
    taps = jnp.transpose(middle_weight, (0, 1, 3, 2)).reshape(3, 3 * inner, inner)

    act = jnp.pad(jnp.maximum(first_pre, 0), ((1, 1), (1, 1), (0, 0)))
    act = jnp.concatenate(beside(act), axis=2)
    act_a, act_b = act[:, :split], act[:, split:]
    rim_act = jnp.concatenate([act[1:2], act[-2:-1]], axis=0)
    lw0 = jnp.zeros((channels // LANES, inner, LANES), F32)
    mw0 = jnp.zeros((3, inner, 3 * inner), F32)
    fw0 = jnp.zeros((inner, channels), F32)

    (send_b, lane_sort, pixel_sort, taps, act_a, act_b, rim_act, lw0, mw0, fw0) = (
        lax.optimization_barrier(
            (send_b, lane_sort, pixel_sort, taps, act_a, act_b, rim_act, lw0, mw0, fw0)
        )
    )
    recv_b = exchange(send_b)
    sorts = (lane_sort, pixel_sort)

    buf, sg_a, lw = open_block(
        None, recv_a, output_pre, second_pre, *sorts, last_weight, lw0, join, 0
    )
    mw = middle(sg_a, act_a, mw0)
    left = jnp.pad(sg_a, ((0, 0), (1, 0), (0, 0)))
    buf, fw = close_block(
        buf,
        sorted_taps(left, seam),
        taps,
        first_pre,
        block_input,
        first_weight,
        fw0,
        0,
    )

    lw, mw, fw = lax.optimization_barrier((lw, mw, fw))
    buf, sg_b, lw = open_block(
        buf, recv_b, output_pre, second_pre, *sorts, last_weight, lw, join, head
    )
    first, last = [
        jnp.concatenate([sg_a[e : e + 1], sg_b[e : e + 1]], axis=1)
        for e in (0, tile_rows - 1)
    ]
    before, after = edges(first, last, count)
    mw = middle(sg_b, act_b, mw)
    both = add_rims(mw, lw, before[0], after[0], rim_act)

    size = both.shape[0] // count
    part, fw, sg_b = lax.optimization_barrier(
        (both.reshape(count, size, LANES), fw, sg_b)
    )
    parts = exchange(part).astype(F32)
    share = (jnp.sum(parts, axis=0) * factor).astype(BF)

    far = jnp.concatenate([sg_a[:, seam - 1 :], sg_b], axis=1)
    far = jnp.pad(far, ((0, 0), (0, 1), (0, 0)))
    buf, fw = close_block(
        buf,
        sorted_taps(far, map_cols - seam),
        taps,
        first_pre,
        block_input,
        first_weight,
        fw,
        closed,
    )
    low = jnp.concatenate([sg_a[:2], sg_b[:2]], axis=1)
    high = jnp.concatenate([sg_a[-2:], sg_b[-2:]], axis=1)
    rim = jnp.concatenate([before, low, high, after], axis=0)
    rim = sorted_taps(jnp.pad(rim, ((0, 0), (1, 1), (0, 0))), map_cols)
    buf, fw = close_edges(
        buf,
        rim.reshape(2, 3, map_cols, 3 * inner),
        taps,
        first_pre,
        block_input,
        first_weight,
        fw,
    )
    chips = count // 2
    got = exchange_chips(
        jnp.concatenate(
            [
                jnp.broadcast_to(share[None], (chips, size, LANES)),
                fw.reshape(chips, 2 * own, LANES),
            ],
            axis=1,
        ),
        count,
    )
    other = swap_cores(got, count)
    middle_wgrad, last_wgrad, first_wgrad = finish(
        (lax.axis_index(AXIS) % 2).reshape(1), got, other, size, factor, inner, channels
    )
    return (buf, first_wgrad, middle_wgrad.reshape(3, 3, inner, inner), last_wgrad)


def solution(mesh):
    placed = (
        P(("groups", "rows"), None, None),
        P(("groups", "rows"), None, None),
        P(("groups", "rows"), None, None),
        P(("groups", "rows"), None, None),
        P("groups", None, "rows"),
        P(),
        P(),
        P(),
    )
    return jax.shard_map(
        shards,
        mesh=mesh,
        in_specs=placed,
        out_specs=(
            P(("groups", "rows"), None, None),
            P(("groups", "rows"), None),
            P("groups", None, None, None),
            P("groups", None),
        ),
        check_vma=False,
    )
```
